512 devices in a mesh: ctx: 64 (over z, y), tp: 4 (over x), dp: 2 (over core).
Axes of the slice: x: 4, y: 8, z: 8, core: 2. Of those that a mesh axis runs over, the one named last changes fastest.
Arguments:
- projected: bfloat16 [3, 2, 16384, 1024], P(None, 'dp', 'ctx', 'tp'), may hold values from -6 to 6
- segment_ids: int32 [2, 16384], P('dp', 'ctx'), may hold values from 0 to 31, never falling along the last dimension, each value on 1 to 768 neighbouring positions
- short_filter: float32 [3, 3, 1024], P(None, None, 'tp'), may hold values from -3.5 to 3.5
- long_filter: float32 [64, 16384], P('tp', 'ctx'), may hold values from -4 to 4
- out_proj: bfloat16 [1024, 1024], P('tp'), may hold values from -0.1875 to 0.1875
- mixed_cotangent: bfloat16 [2, 16384, 1024], P('dp', 'ctx', 'tp'), may hold values from -6 to 6
Outputs:
- mixed: bfloat16 [2, 16384, 1024], P('dp', 'ctx', 'tp')
- grad_projected: bfloat16 [3, 2, 16384, 1024], P(None, 'dp', 'ctx', 'tp')
- grad_short: float32 [3, 3, 1024], P(None, None, 'tp')
- grad_long: float32 [64, 16384], P('tp', 'ctx')
- grad_out_proj: float32 [1024, 1024], P('tp')
The draws below stay inside these ranges and needn't reach their ends.
Inputs may be any that keep to these rules, and one draw needn't show every extreme that they name: `segment_ids`: along each window the id never falls; every id covers 1 to 768 consecutive positions, and one covers exactly 768.
All inputs are finite; a program needn't handle non-finite values.
Results may differ from the reference program's by a relative error of at most 0.0049.
Values may be sent and summed in bfloat16 or wider, within the bound.
A program may use at most 64 MiB of HBM per device.

```python
import math
import jax
import jax.numpy as jnp
import numpy as np
from jax import lax

CH = 1024
GROUP = 16
SHORT = 3
LEN_DEV = 256
PACKED_SPAN = 16384
SEQS = 2
KERNEL_SETS = 64
DOCS = 32


def draw_long_filter(key, part):
    fraction_seed_handle, jitter_seed_handle, cluster_seed_handle = jax.random.split(jax.random.fold_in(key, 17), 3)
    removal_sites = jnp.arange(PACKED_SPAN, dtype=jnp.float32)[None, :]
    rates = jnp.exp(jax.random.uniform(fraction_seed_handle, (KERNEL_SETS, 1), jnp.float32, math.log(0.5 / PACKED_SPAN), math.log(1.0 / 30.0)))
    noise = jnp.clip(jax.random.normal(jitter_seed_handle, (KERNEL_SETS, PACKED_SPAN), jnp.float32), -4.0, 4.0)
    scaling = jnp.sqrt((1.0 - jnp.exp(-2.0 * rates)) / (1.0 - jnp.exp(-2.0 * rates * PACKED_SPAN)))
    cluster_extents = jax.random.randint(cluster_seed_handle, (3, KERNEL_SETS, 1), 0, PACKED_SPAN).astype(jnp.float32)
    removed_symbols = jnp.prod(jnp.where(removal_sites[None] >= cluster_extents, 0.65, 1.0), axis=0)
    return (scaling * jnp.exp(-rates * removal_sites) * removed_symbols * noise).astype(jnp.float32)


def level_of(key, dims, shards, least, top_value):
    factor_of = 1.0
    for axis_at, shards_of in shards:
        heights = jax.random.uniform(jax.random.fold_in(jax.random.fold_in(key, 6), axis_at), (shards_of,), jnp.float32, least / len(shards), top_value / len(shards))
        factor_of = factor_of * jnp.repeat(jnp.exp(heights), dims[axis_at] // shards_of).reshape((-1,) + (1,) * (len(dims) - 1 - axis_at))
    return factor_of


def split_up(number_of, total, bound, skew):
    loads = [(1 << 20) // math.isqrt(grade ** skew) + 1 for grade in range(2, number_of + 1)]
    spare, counts = total - bound - (number_of - 1), [1] * (number_of - 1)
    while spare > 0:
        candidates = [i for i in range(number_of - 1) if counts[i] < bound]
        pool, remaining = sum([loads[i] for i in candidates]), spare
        for i in candidates:
            addition = min(bound - counts[i], max(1, remaining * loads[i] // pool), spare)
            counts[i] = counts[i] + addition
            spare = spare - addition
    return np.array([bound] + counts)


def ragged_sizes(own_key, number_of, total, bound, lean):
    if number_of == 2:
        one = jax.random.randint(own_key, (), max(1, total - bound), min(bound, total - 1) + 1)
        return jnp.stack([one, total - one])
    tallies = jnp.asarray(split_up(number_of, total, bound, lean), jnp.int32)
    pairs = (number_of - 1) // 2
    donor, sink = tallies[1:1 + 2 * pairs:2], tallies[2:2 + 2 * pairs:2]
    room = jnp.minimum(donor - 1, bound - sink)
    shifted = jax.random.randint(jax.random.fold_in(own_key, 1), (pairs,), 0, 1 << 20) % (room + 1)
    tallies = tallies.at[1:1 + 2 * pairs:2].set(donor - shifted).at[2:2 + 2 * pairs:2].set(sink + shifted)
    return tallies[jax.random.permutation(jax.random.fold_in(own_key, 2), number_of)]


def normal_values(rng, shape, spread, limit, pieces=(), kind=jnp.bfloat16):
    result = spread * jax.random.normal(rng, shape, jnp.float32)
    if pieces:
        result = result * level_of(rng, shape, pieces, -0.22, 0.18)
    return jnp.clip(result, -limit, limit).astype(kind)


def setup_inputs(seed: int = 0) -> dict:
    keys = jax.random.split(jax.random.key(seed), 7)
    return {
        "projected": normal_values(keys[0], (3, SEQS, PACKED_SPAN, CH), 1.0, 6.0, ((1, 2), (2, 64), (3, 4))),
        "segment_ids": jax.vmap(lambda own: jnp.searchsorted(jnp.cumsum(ragged_sizes(own, DOCS, PACKED_SPAN, 3 * LEN_DEV, 0)), jnp.arange(PACKED_SPAN), side="right"))(jax.random.split(keys[1], SEQS)).reshape((SEQS, PACKED_SPAN)).astype(jnp.int32),
        "short_filter": normal_values(keys[2], (3, SHORT, CH), SHORT ** -0.5, 3.5, ((2, 4),), jnp.float32),
        "long_filter": draw_long_filter(jax.random.fold_in(keys[6], 71), 0),
        "out_proj": normal_values(keys[4], (CH, CH), CH ** -0.5, 0.1875, ((0, 4),)),
        "mixed_cotangent": normal_values(keys[5], (SEQS, PACKED_SPAN, CH), 1.0, 6.0, ((0, 2), (1, 64), (2, 4))),
    }


def tap_mask(segments, shift_by):
    length = segments.shape[1]
    removal_sites = jnp.arange(length, dtype=jnp.int32)
    earlier = jnp.roll(segments, shift_by, axis=1)
    return jnp.where((removal_sites >= shift_by)[None, :] & (earlier == segments), 1.0, 0.0).astype(jnp.float32)

def short_forward(inputs, filters, segments):
    running = jnp.zeros_like(inputs)
    for shift_by in range(filters.shape[1]):
        valid_mask = tap_mask(segments, shift_by)
        running = running + filters[:, shift_by][:, None, None, :] * valid_mask[None, :, :, None] * jnp.roll(inputs, shift_by, axis=2)
    return running

def short_backward(inputs, filters, segments, cotangent):
    pulled = jnp.zeros_like(cotangent)
    tap_rows = []
    for shift_by in range(filters.shape[1]):
        masked = cotangent * tap_mask(segments, shift_by)[None, :, :, None]
        pulled = pulled + filters[:, shift_by][:, None, None, :] * jnp.roll(masked, -shift_by, axis=2)
        tap_rows.append(lax.optimization_barrier(jnp.sum(masked * jnp.roll(inputs, shift_by, axis=2), axis=(1, 2))))
    return (pulled, jnp.stack(tap_rows, axis=1))

def reference(projected, segment_ids, short_filter, long_filter, out_proj, mixed_cotangent):
    grad_scale = 1.0 / math.sqrt(SEQS * PACKED_SPAN)
    inputs = projected.astype(jnp.float32)
    short_out = short_forward(inputs, short_filter, segment_ids)
    gated_rows = short_out[1] * short_out[2]
    fft_length = 2 * PACKED_SPAN
    mid_spec = jnp.fft.rfft(gated_rows, n=fft_length, axis=1)
    filt_spec = jnp.fft.rfft(jnp.repeat(long_filter.T, GROUP, axis=1), n=fft_length, axis=0)
    long_out = jnp.fft.irfft(mid_spec * filt_spec[None], n=fft_length, axis=1)[:, :PACKED_SPAN]
    y_out = (short_out[0] * long_out).astype(jnp.bfloat16)
    flat_y = y_out.reshape(SEQS * PACKED_SPAN, CH)
    flat_cot = mixed_cotangent.reshape(SEQS * PACKED_SPAN, CH)
    mixed = jnp.dot(flat_y, out_proj, preferred_element_type=jnp.float32).astype(jnp.bfloat16).reshape(SEQS, PACKED_SPAN, CH)
    grad_y = jnp.dot(flat_cot, out_proj.T, preferred_element_type=jnp.float32).reshape(SEQS, PACKED_SPAN, CH)
    grad_out_proj = jnp.dot(flat_y.T, flat_cot, preferred_element_type=jnp.float32) * grad_scale
    grad_long_out = grad_y * short_out[0]
    grad_query = grad_y * long_out
    cot_spec = jnp.fft.rfft(grad_long_out, n=fft_length, axis=1)
    grad_gated = jnp.fft.irfft(jnp.conj(filt_spec)[None] * cot_spec, n=fft_length, axis=1)[:, :PACKED_SPAN]
    cross_spec = lax.optimization_barrier(jnp.sum(jnp.conj(mid_spec) * cot_spec, axis=0)).reshape(PACKED_SPAN + 1, KERNEL_SETS, GROUP).sum(axis=2)
    grad_long = jnp.fft.irfft(cross_spec, n=fft_length, axis=0)[:PACKED_SPAN].T * grad_scale
    grad_short_out = jnp.stack([grad_query, grad_gated * short_out[2], grad_gated * short_out[1]])
    grad_inputs, tap_sums = short_backward(inputs, short_filter, segment_ids, grad_short_out)
    return (mixed, grad_inputs.astype(jnp.bfloat16), tap_sums * grad_scale, grad_long, grad_out_proj)
```

```python
import functools
import math

import jax
import jax.numpy as jnp
from jax import lax
from jax.experimental import pallas as pl
from jax.experimental.pallas import tpu as pltpu
from jax.sharding import PartitionSpec as P

F32 = jnp.float32
BF = jnp.bfloat16
MESH = pl.DeviceIdType.MESH


def shifted(value, axis, steps):
    count = lax.axis_size(axis)
    first, last = (max(0, -steps), min(count, count - steps))
    return lax.ppermute(value, axis, [(source, source + steps) for source in range(first, last)])


def short_local(extended, filters, seg_ext):
    reach_taps = filters.shape[1]
    out_rows = extended.shape[1] - reach_taps + 1
    own_seg = seg_ext[reach_taps - 1 :]
    running = jnp.zeros((extended.shape[0], out_rows, extended.shape[2]), jnp.float32)
    for shift_by in range(reach_taps):
        start_row = reach_taps - 1 - shift_by
        same_doc = jnp.where(seg_ext[start_row : start_row + out_rows] == own_seg, 1.0, 0.0)
        running = (
            running
            + filters[:, shift_by][:, None, :]
            * same_doc[None, :, None]
            * extended[:, start_row : start_row + out_rows]
        )
    return running


def conv_kernel(x_ref, h_ref, out_ref, gl_ref, tt, lb, acc, gt, xb0, xb1, dd, hi):
    row = lax.broadcasted_iota(jnp.int32, (128, 128), 0)
    col = lax.broadcasted_iota(jnp.int32, (128, 128), 1)
    upper = col >= row

    def spread(e):
        return pltpu.roll(jnp.broadcast_to(h_ref[pl.ds(e, 1), :], (128, 128)), 0, 1, stride=1, stride_axis=0)

    def build(d, prev):
        s0 = spread(2 * d)
        a0 = jnp.where(upper, s0, prev).astype(BF)
        s1 = spread(2 * d + 1)
        a1 = jnp.where(upper, s1, s0).astype(BF)
        base = pl.multiple_of(d * 256, 256)
        tt[pl.ds(base, 128), 0:128] = a0
        tt[pl.ds(base + 128, 128), 128:256] = a0
        tt[pl.ds(base, 128), 128:256] = a1
        tt[pl.ds(base + 384, 128), 0:128] = a1
        return s1

    tt[128:256, 0:128] = jnp.zeros((128, 128), BF)
    lax.fori_loop(0, 64, build, jnp.zeros((128, 128), F32))

    x = x_ref[...].astype(F32).reshape(512, 256)
    first = lax.broadcasted_iota(jnp.int32, (8, 256), 0) < 4
    zero8 = jnp.zeros((8, 256), F32)
    mixed = jnp.concatenate(
        [jnp.where(first, x[8 * k : 8 * k + 8], x[504 - 8 * k : 512 - 8 * k]) for k in range(64)], axis=0
    )
    for e in range(4):
        if e:
            lb[:, 256 * e : 256 * e + 256] = jnp.concatenate(
                [jnp.zeros((8 * e, 256), F32), mixed[: 512 - 8 * e]], axis=0
            ).astype(BF)
        else:
            lb[:, 0:256] = mixed.astype(BF)
    for step in range(16):
        part = jnp.dot(lb[0 : 512 - 32 * step, :], tt[1024 * step : 1024 * step + 1024, :], preferred_element_type=F32)
        if step:
            acc[32 * step : 512, :] += part
        else:
            acc[...] = part
    for k in range(64):
        out_ref[k] = jnp.where(first, acc[8 * k : 8 * k + 8, :], acc[504 - 8 * k : 512 - 8 * k, :]).astype(BF)

    firsts = lax.rem(lax.broadcasted_iota(jnp.int32, (512, 256), 0), 8) < 4
    gt[...] = jnp.transpose(jnp.where(firsts, x, 0.0)).astype(BF)
    swapped = x
    moved = jnp.concatenate([x[4:], jnp.zeros((4, 256), F32)], axis=0)
    xb0[0:512, :] = moved.astype(BF)
    xb0[512:640, :] = jnp.zeros((128, 256), BF)
    xb1[0:512, :] = jnp.concatenate([moved[8:], zero8], axis=0).astype(BF)
    xb1[512:640, :] = jnp.zeros((128, 256), BF)
    dd[...] = jnp.zeros(dd.shape, F32)

    def corr(d, width, src, off):
        c = jnp.dot(gt[:, 0:width], src[pl.ds(pl.multiple_of(off, 16), width), :], preferred_element_type=F32)
        base = pl.multiple_of(d * 256, 256)
        dd[pl.ds(base, 128), :] += c[128:256, 128:256]
        dd[pl.ds(base + 128, 128), :] = c[0:128, 128:256] + c[128:256, 0:128]
        dd[pl.ds(base + 256, 128), :] = c[0:128, 0:128]

    for seg in range(4):
        width = 512 - 128 * seg

        def pair(i, carry, seg=seg, width=width):
            d = 16 * seg + 2 * i
            corr(d, width, xb0, 8 * d)
            corr(d + 1, width, xb1, 8 * d)
            return carry

        lax.fori_loop(0, 8, pair, 0)

    def fold(e, carry):
        rolled = pltpu.roll(dd[pl.ds(pl.multiple_of(e * 128 + 128, 128), 128), :], 0, 1, stride=1, stride_axis=0)
        low = jnp.where(upper, rolled, 0.0)
        gl_ref[pl.ds(e, 1), :] = jnp.sum(low, axis=0, keepdims=True)
        hi[pl.ds(e, 1), :] = jnp.sum(rolled - low, axis=0, keepdims=True)
        return carry

    hi[128:136, :] = jnp.zeros((8, 128), F32)
    lax.fori_loop(0, 128, fold, 0)
    gl_ref[...] += hi[1:129, :]


def conv(x, h):
    return pl.pallas_call(
        conv_kernel,
        out_shape=(jax.ShapeDtypeStruct((64, 8, 256), BF), jax.ShapeDtypeStruct((128, 128), F32)),
        in_specs=[pl.BlockSpec(memory_space=pltpu.VMEM)] * 2,
        out_specs=[pl.BlockSpec(memory_space=pltpu.VMEM)] * 2,
        scratch_shapes=[
            pltpu.VMEM((64 * 256 + 256, 256), BF),
            pltpu.VMEM((512, 1024), BF),
            pltpu.VMEM((512, 256), F32),
            pltpu.VMEM((256, 512), BF),
            pltpu.VMEM((640, 256), BF),
            pltpu.VMEM((640, 256), BF),
            pltpu.VMEM((130 * 128, 128), F32),
            pltpu.VMEM((136, 128), F32),
        ],
        compiler_params=pltpu.CompilerParams(vmem_limit_bytes=40 << 20),
        name="conv",
    )(x, h)


def reduce_kernel(scale, part_ref, small_ref, out_ref, osmall_ref,
                  pair_out, pair_in, s1, b1_in, s2, b2_in, g2, g1, gp,
                  sp_in, sm0, sm1, sm2, snd, rcv):
    ctx = lax.axis_index("ctx")
    dp = lax.axis_index("dp")
    y = lax.rem(ctx, 8)
    z = ctx // 8
    my1 = y * (1 - dp) + z * dp
    my2 = z * (1 - dp) + y * dp
    step1 = 1 + 7 * dp
    step2 = 8 - 7 * dp
    base1 = ctx - my1 * step1
    base2 = ctx - my2 * step2
    other = 1 - dp

    def peer1(k):
        return lax.rem(my1 + k, 8)

    def dev1(k):
        return {"ctx": base1 + peer1(k) * step1}

    def peer2(k):
        return lax.rem(my2 + k, 8)

    def dev2(k):
        return {"ctx": base2 + peer2(k) * step2}

    barrier = pltpu.get_barrier_semaphore()
    pl.semaphore_signal(barrier, 1, device_id={"dp": other}, device_id_type=MESH)
    for k in range(1, 8):
        pl.semaphore_signal(barrier, 1, device_id=dev1(k), device_id_type=MESH)
        pl.semaphore_signal(barrier, 1, device_id=dev2(k), device_id_type=MESH)
    pl.semaphore_wait(barrier, 15)

    def copy(src, dst, n, dev):
        return pltpu.make_async_remote_copy(src, dst, snd.at[n], rcv.at[n], device_id=dev, device_id_type=MESH)

    off = pl.multiple_of(other * 128, 128)
    mine = pl.multiple_of(dp * 128, 128)
    pair_out[...] = part_ref[pl.ds(off, 128), :].astype(BF)
    sm0[0] = small_ref[...]
    c0 = copy(pair_out, pair_in, 0, {"dp": other})
    c0.start()
    c1 = copy(sm0.at[0], sm0.at[1], 1, {"dp": other})
    c1.start()
    c1.wait()
    c0.wait()
    s1[...] = (part_ref[pl.ds(mine, 128), :] + pair_in[...].astype(F32)).astype(BF)
    sm1[0] = sm0[0] + sm0[1]

    def rows(k):
        return pl.ds(pl.multiple_of(k * 16, 16), 16)

    def cols(k):
        return pl.ds(pl.multiple_of(k * 128, 128), 128)

    cs = []
    for k in range(1, 8):
        c = copy(s1.at[rows(peer1(k)), :], b1_in.at[k], 1 + k, dev1(k)); c.start(); cs.append(c)
        c = copy(sm1.at[0], sm1.at[k], 8 + k, dev1(k)); c.start(); cs.append(c)
    for c in cs:
        c.wait()
    tot = s1[rows(my1), :].astype(F32)
    small = sm1[0]
    for k in range(1, 8):
        tot += b1_in[k].astype(F32)
    for k in range(1, 8):
        small += sm1[k]
    s2[...] = tot.astype(BF)
    sm2[0] = small
    cs = []
    for k in range(1, 8):
        c = copy(s2.at[:, cols(peer2(k))], b2_in.at[k], 15 + k, dev2(k)); c.start(); cs.append(c)
        c = copy(sm2.at[0], sm2.at[k], 22 + k, dev2(k)); c.start(); cs.append(c)
    for c in cs:
        c.wait()
    tot = s2[:, cols(my2)].astype(F32)
    small = sm2[0]
    for k in range(1, 8):
        tot += b2_in[k].astype(F32)
    for k in range(1, 8):
        small += sm2[k]
    osmall_ref[...] = small * scale
    g2[:, cols(my2)] = (tot * scale).astype(BF)
    cs = []
    for k in range(1, 8):
        c = copy(g2.at[:, cols(my2)], g2.at[:, cols(my2)], 29 + k, dev2(k)); c.start(); cs.append(c)
    for c in cs:
        c.wait()
    g1[rows(my1), :] = g2[...]
    cs = []
    for k in range(1, 8):
        c = copy(g1.at[rows(my1), :], g1.at[rows(my1), :], 36 + k, dev1(k)); c.start(); cs.append(c)
    for c in cs:
        c.wait()
    c0 = copy(g1, gp, 44, {"dp": other})
    c0.start()
    out_ref[pl.ds(mine, 128), :] = g1[...].astype(F32)
    c0.wait()
    out_ref[pl.ds(off, 128), :] = gp[...].astype(F32)


def reduce_all(part, small, scale):
    return pl.pallas_call(
        functools.partial(reduce_kernel, scale),
        out_shape=(jax.ShapeDtypeStruct((256, 1024), F32), jax.ShapeDtypeStruct((16, 256), F32)),
        in_specs=[pl.BlockSpec(memory_space=pltpu.VMEM)] * 2,
        out_specs=[pl.BlockSpec(memory_space=pltpu.VMEM)] * 2,
        scratch_shapes=[
            pltpu.VMEM((128, 1024), BF), pltpu.VMEM((128, 1024), BF), pltpu.VMEM((128, 1024), BF),
            pltpu.VMEM((8, 16, 1024), BF), pltpu.VMEM((16, 1024), BF), pltpu.VMEM((8, 16, 128), BF),
            pltpu.VMEM((16, 1024), BF), pltpu.VMEM((128, 1024), BF), pltpu.VMEM((128, 1024), BF),
            pltpu.VMEM((8, 128), F32), pltpu.VMEM((2, 16, 256), F32), pltpu.VMEM((8, 16, 256), F32), pltpu.VMEM((8, 16, 256), F32),
            pltpu.SemaphoreType.DMA((45,)), pltpu.SemaphoreType.DMA((45,)),
        ],
        compiler_params=pltpu.CompilerParams(vmem_limit_bytes=24 << 20, collective_id=0, has_side_effects=True),
        name="reduce_all",
    )(part, small)


def lanes_first(block):
    return block.T.reshape(64, 4, 256)


def per_device(projected, segment_ids, short_filter, long_filter, out_proj, mixed_cotangent):
    grad_scale = 1.0 / math.sqrt(2 * 256 * lax.axis_size("ctx"))
    segments = segment_ids[0]
    source = projected[:, 0]
    cot_full = lax.all_gather(mixed_cotangent[0], "tp", axis=1, tiled=True)
    filter_rows = lax.all_to_all(jnp.repeat(long_filter.astype(BF), 4, axis=0), "ctx", 0, 0, tiled=True)
    prev_tail, prev_seg = shifted((source[:, 254:], segments[254:]), "ctx", 1)
    short_seg = jnp.concatenate([prev_seg, segments])
    short_ext = jnp.concatenate([prev_tail, source], axis=1).astype(F32)
    short_out, short_pull = jax.vjp(lambda e, f: short_local(e, f, short_seg), short_ext, short_filter)
    query_conv = short_out[0]
    gated_rows = (short_out[1] * short_out[2]).astype(BF)
    grad_y = lax.dot_general(cot_full, out_proj, (((1,), (1,)), ((), ())), preferred_element_type=F32)
    grad_long_out = (grad_y * query_conv).astype(BF)
    sent = jnp.concatenate([lanes_first(gated_rows), lanes_first(grad_long_out[::-1])], axis=1)
    got = lax.all_to_all(sent, "ctx", 0, 0, tiled=True)
    conv_out, long_part = conv(got, filter_rows.astype(F32).reshape(128, 128))
    back = lax.all_to_all(conv_out, "ctx", 0, 0, tiled=True)
    long_back = lax.all_to_all(long_part.reshape(64, 256).astype(BF), "ctx", 0, 0, tiled=True)
    long_out = back[:, :4].reshape(256, 256).T.astype(F32)
    grad_gated = back[:, 4:].reshape(256, 256).T[::-1].astype(F32)
    grad_long_local = long_back.astype(F32).reshape(16, 4, 2, 128).sum(axis=1)[:, :, ::-1].reshape(16, 256)
    y_out = (query_conv * long_out).astype(BF)
    partial_out = jnp.dot(y_out, out_proj, preferred_element_type=F32)
    mixed = lax.psum_scatter(partial_out, "tp", scatter_dimension=1, tiled=True).astype(BF)
    grad_proj_local = jnp.dot(y_out.T, cot_full, preferred_element_type=F32)
    grad_query = grad_y * long_out
    grad_short_out = jnp.stack([grad_query, grad_gated * short_out[2], grad_gated * short_out[1]])
    grad_short_ext, grad_short_local = short_pull(grad_short_out)
    returned_short = shifted(grad_short_ext[:, :2], "ctx", -1)
    grad_source = grad_short_ext[:, 2:] + jnp.concatenate([jnp.zeros((3, 254, 256), F32), returned_short], axis=1)
    small = jnp.concatenate([grad_short_local.reshape(9, 256), jnp.zeros((7, 256), F32)], axis=0)
    total_proj, total_small = reduce_all(grad_proj_local, small, grad_scale)
    total_long = lax.psum(grad_long_local, "dp")
    return (
        mixed[None],
        grad_source[:, None].astype(BF),
        total_small[:9].reshape(3, 3, 256),
        total_long * grad_scale,
        total_proj,
    )


def solution(mesh):
    in_specs = (
        P(None, "dp", "ctx", "tp"),
        P("dp", "ctx"),
        P(None, None, "tp"),
        P("tp", "ctx"),
        P("tp", None),
        P("dp", "ctx", "tp"),
    )
    out_specs = (
        P("dp", "ctx", "tp"),
        P(None, "dp", "ctx", "tp"),
        P(None, None, "tp"),
        P("tp", "ctx"),
        P("tp", None),
    )
    return jax.shard_map(
        per_device, mesh=mesh, in_specs=in_specs, out_specs=out_specs, check_vma=False
    )
```

```python
import functools
import math

import jax
import jax.numpy as jnp
from jax import lax
from jax.experimental import pallas as pl
from jax.experimental.pallas import tpu as pltpu
from jax.sharding import PartitionSpec as P

F32 = jnp.float32
BF = jnp.bfloat16
MESH = pl.DeviceIdType.MESH
CTX = 64
TP = 4
TAPS = 3
ROWS = 256
COLS = 256
HALF = 128


def iota(shape, axis):
    return lax.broadcasted_iota(jnp.int32, shape, axis)


def one_hot(condition):
    return jnp.where(condition, 1.0, 0.0).astype(BF)


def across(a, b):
    return lax.dot_general(a, b, (((1,), (1,)), ((), ())), preferred_element_type=F32)


def plain(a, b):
    return jnp.dot(a, b, preferred_element_type=F32)


def layer(
    scale,
    x_ref, seg_ref, taps_ref, filt_ref, w_ref, cot_ref,
    mixed_ref, gin_ref, gtaps_ref, glong_ref, gproj_ref,
    cot_all, halo_out, halo_in, filt_out, filt_in, xe, so, masks, gy,
    send, recv, toep, stacked, acc, gct, gls, lag_out, lag_in,
    ret, back, zbuf, part, mix_out, mix_in,
    pair_out, pair_in, s1, b1_in, s2, b2_in, g2, g1, gp,
    sm0, sm1, sm2, edge_out, edge_in, lag_pair,
    snd, rcv, all_snd, all_rcv,
):
    ctx = lax.axis_index("ctx")
    tp = lax.axis_index("tp")
    dp = lax.axis_index("dp")
    y = lax.rem(ctx, 8)
    z = ctx // 8
    my1 = y * (1 - dp) + z * dp
    my2 = z * (1 - dp) + y * dp
    step1 = 1 + 7 * dp
    step2 = 8 - 7 * dp
    base1 = ctx - my1 * step1
    base2 = ctx - my2 * step2
    other = 1 - dp

    def peer1(k):
        return lax.rem(my1 + k, 8)

    def dev1(k):
        return {"ctx": base1 + peer1(k) * step1}

    def peer2(k):
        return lax.rem(my2 + k, 8)

    def dev2(k):
        return {"ctx": base2 + peer2(k) * step2}

    def peer_tp(k):
        return lax.rem(tp + k, TP)

    def peer_ctx(k):
        return lax.rem(ctx + k, CTX)

    def copy(src, dst, n, dev):
        return pltpu.make_async_remote_copy(
            src, dst, snd.at[n], rcv.at[n], device_id=dev, device_id_type=MESH
        )

    barrier = pltpu.get_barrier_semaphore()

    def greet(k, carry):
        pl.semaphore_signal(barrier, 1, device_id={"ctx": peer_ctx(k)}, device_id_type=MESH)
        return carry

    for k in range(1, TP):
        pl.semaphore_signal(barrier, 1, device_id={"tp": peer_tp(k)}, device_id_type=MESH)
    pl.semaphore_signal(barrier, 1, device_id={"dp": other}, device_id_type=MESH)
    lax.fori_loop(1, CTX, greet, 0)

    rows128 = iota((HALF, HALF), 0)
    cols128 = iota((HALF, HALF), 1)
    flip128 = one_hot(rows128 + cols128 == HALF - 1)
    filt = filt_ref[...].astype(BF)
    filt_out[...] = jnp.concatenate(
        [plain(filt[:, :HALF], flip128), plain(filt[:, HALF:], flip128)], axis=1
    ).reshape(16, 1, COLS)
    seg_row = seg_ref[...].astype(F32)
    seg_col = jnp.transpose(jnp.broadcast_to(seg_row, (HALF, ROWS)))
    halo_out[0:6, :] = jnp.concatenate([x_ref[i, ROWS - 2 : ROWS, :].astype(F32) for i in range(3)], axis=0)
    halo_out[6:8, :] = jnp.concatenate([seg_col[ROWS - 2 : ROWS, :]] * 2, axis=1)
    pl.semaphore_wait(barrier, CTX - 1 + TP - 1 + 1)

    halo = copy(halo_out, halo_in, 0, {"ctx": peer_ctx(1)})
    halo.start()
    cot_copies = []
    for k in range(1, TP):
        c = copy(cot_ref, cot_all.at[tp], k, {"tp": peer_tp(k)})
        c.start()
        cot_copies.append(c)

    def send_filter(k, carry):
        peer = peer_ctx(k)
        pltpu.make_async_remote_copy(
            filt_out.at[peer // 4], filt_in.at[ctx], all_snd.at[0], all_rcv.at[0],
            device_id={"ctx": peer}, device_id_type=MESH,
        ).start()
        return carry

    lax.fori_loop(1, CTX, send_filter, 0)
    filt_in[pl.ds(ctx, 1)] = filt_out[pl.ds(ctx // 4, 1)]
    cot_all[pl.ds(tp, 1)] = cot_ref[...].reshape(1, ROWS, COLS)

    def wait_all(buf, n, which):
        pltpu.make_async_copy(buf.at[pl.ds(0, CTX - 1)], buf.at[pl.ds(0, CTX - 1)], which.at[n]).wait()

    for i in range(3):
        xe[i, 8 : 8 + ROWS, :] = x_ref[i].astype(F32)
    halo.wait()

    for i in range(3):
        xe[i, 6:8, :] = halo_in[2 * i : 2 * i + 2, :]
    prev_seg = jnp.where(ctx == 0, -1.0, halo_in[6:8, 0:HALF])
    before1 = jnp.concatenate([prev_seg[1:2], seg_col[: ROWS - 1]], axis=0)
    before2 = jnp.concatenate([prev_seg, seg_col[: ROWS - 2]], axis=0)
    for n, before in enumerate((before1, before2)):
        mask = jnp.where(before == seg_col, 1.0, 0.0)
        masks[n] = jnp.concatenate([mask, mask], axis=1)
    for i in range(3):
        so[i] = (
            taps_ref[i, 0:1, :] * xe[i, 8 : 8 + ROWS, :]
            + taps_ref[i, 1:2, :] * masks[0] * xe[i, 7 : 7 + ROWS, :]
            + taps_ref[i, 2:3, :] * masks[1] * xe[i, 6 : 6 + ROWS, :]
        )

    wait_all(filt_in, 0, all_rcv)
    keep = rows128 >= cols128

    def spread(line):
        return pltpu.roll(jnp.broadcast_to(line, (HALF, HALF)), 1, 1, stride=1, stride_axis=0)

    def build(n, prev):
        for u in range(2):
            d = 2 * n + u
            line = filt_in[d]
            s0 = spread(line[:, :HALF])
            a0 = jnp.where(keep, s0, prev).astype(BF)
            s1_ = spread(line[:, HALF:])
            a1 = jnp.where(keep, s1_, s0).astype(BF)
            base = pl.multiple_of(d * 256, 256)
            toep[pl.ds(base, HALF), 0:HALF] = a0
            toep[pl.ds(base + HALF, HALF), HALF:COLS] = a0
            toep[pl.ds(base + HALF, HALF), 0:HALF] = a1
            toep[pl.ds(base + 256, HALF), HALF:COLS] = a1
            prev = s1_
        return prev

    toep[0:HALF, HALF:COLS] = jnp.zeros((HALF, HALF), BF)
    lax.fori_loop(0, 32, build, jnp.zeros((HALF, HALF), F32))

    for c in cot_copies:
        c.wait()
    total = across(cot_all[0], w_ref[:, 0:256])
    for i in range(1, TP):
        total += across(cot_all[i], w_ref[:, 256 * i : 256 * i + 256])
    gy[...] = total
    flip = one_hot(iota((ROWS, ROWS), 0) + iota((ROWS, ROWS), 1) == ROWS - 1)
    slot = iota((512, COLS), 0)
    chan = iota((512, COLS), 1)
    home = (slot // 8) * 4 + lax.rem(slot, 8)
    pick_a = one_hot((home == chan) & (lax.rem(slot, 8) < 4))
    pick_b = one_hot((home == chan + 4) & (lax.rem(slot, 8) >= 4))
    gated = (so[1] * so[2]).astype(BF)
    gated_back = plain(flip, gated).astype(BF)
    glo = (total * so[0]).astype(BF)
    send[...] = (across(pick_a, gated_back) + across(pick_b, glo)).reshape(CTX, 8, ROWS).astype(BF)

    def scatter(src, dst, n):
        def one(k, carry):
            peer = peer_ctx(k)
            pltpu.make_async_remote_copy(
                src.at[peer], dst.at[ctx], all_snd.at[n], all_rcv.at[n],
                device_id={"ctx": peer}, device_id_type=MESH,
            ).start()
            return carry

        lax.fori_loop(1, CTX, one, 0)
        dst[pl.ds(ctx, 1)] = src[pl.ds(ctx, 1)]

    scatter(send, recv, 1)
    wait_all(recv, 1, all_rcv)

    x8 = recv[...].astype(F32)
    first = iota((8, COLS), 0) < 4
    joined = jnp.concatenate([jnp.where(first, x8[k], x8[CTX - 1 - k]) for k in range(CTX)], axis=0)
    for e in range(4):
        if e:
            stacked[:, 256 * e : 256 * e + 256] = jnp.concatenate(
                [jnp.zeros((8 * e, COLS), F32), joined[: 512 - 8 * e]], axis=0
            ).astype(BF)
        else:
            stacked[:, 0:256] = joined.astype(BF)
    for n in range(16):
        term = plain(stacked[0 : 512 - 32 * n, :], toep[1024 * n : 1024 * n + 1024, :])
        if n:
            acc[32 * n : 512, :] += term
        else:
            acc[...] = term
    for k in range(CTX):
        ret[k] = jnp.where(first, acc[8 * k : 8 * k + 8, :], acc[504 - 8 * k : 512 - 8 * k, :]).astype(BF)
    scatter(ret, back, 2)

    pairs = recv[...].astype(F32).reshape(32, 16, COLS)
    even = pairs[:, 0:8]
    odd = pairs[:, 8:16]
    even_r = pltpu.roll(even, 4, 1)
    odd_r = pltpu.roll(odd, 4, 1)
    first3 = iota((32, 8, COLS), 1) < 4
    gct[...] = jnp.transpose(jnp.where(first3, even, odd_r).reshape(256, COLS)).astype(BF)
    straight = jnp.where(first3, even_r, odd).reshape(256, COLS)
    next_even = jnp.concatenate([even[1:], jnp.zeros((1, 8, COLS), F32)], axis=0)
    next_even = jnp.where(iota((32, 8, COLS), 0) < 31, next_even, 0.0)
    crossed = jnp.where(first3, odd_r, next_even).reshape(256, COLS)
    zero8 = jnp.zeros((8, COLS), F32)
    for n, value in enumerate(
        (straight, crossed, jnp.concatenate([straight[8:], zero8], axis=0), jnp.concatenate([crossed[8:], zero8], axis=0))
    ):
        gls[n, 0:256, :] = value.astype(BF)
        gls[n, 256:512, :] = jnp.zeros((256, COLS), BF)
    later = cols128 > rows128

    def roll_up(block):
        return pltpu.roll(block, 1, 1, stride=1, stride_axis=0)

    def lag_row(now, last):
        return jnp.sum(jnp.where(later, now, last), axis=0, keepdims=True).reshape(1, 1, HALF)

    def correlate(width):
        def body(m, carry):
            c11, last = carry
            for u in range(4):
                c = plain(gct[:, 0:width], gls[u, pl.ds(pl.multiple_of(16 * m, 16), width), :])
                r0 = roll_up(c11 + c[:HALF, :HALF])
                r1 = roll_up(c[:HALF, HALF:] + c[HALF:, :HALF])
                lag_out[pl.ds(8 * m + 2 * u, 1)] = lag_row(r0, last)
                lag_out[pl.ds(8 * m + 2 * u + 1, 1)] = lag_row(r1, r0)
                c11 = c[HALF:, HALF:]
                last = r1
            return c11, last

        return body

    nothing = jnp.zeros((HALF, HALF), F32)
    carry = lax.fori_loop(0, 8, correlate(256), (nothing, nothing))
    c11, last = lax.fori_loop(8, 16, correlate(128), carry)
    r0 = roll_up(c11)
    lag_out[128:129] = lag_row(r0, last)
    lag_out[129:130] = lag_row(nothing, r0)

    def send_lags(k, carry):
        peer = peer_ctx(k)
        pltpu.make_async_remote_copy(
            lag_out.at[pl.ds(2 * peer + 2, 2)], lag_in.at[ctx], all_snd.at[3], all_rcv.at[3],
            device_id={"ctx": peer}, device_id_type=MESH,
        ).start()
        return carry

    lax.fori_loop(1, CTX, send_lags, 0)
    lag_in[pl.ds(ctx, 1)] = lag_out[pl.ds(2 * ctx + 2, 2)].reshape(1, 2, 1, HALF)

    wait_all(back, 2, all_rcv)
    got = back[...].astype(F32).reshape(512, ROWS).astype(BF)
    slot_t = iota((COLS, 512), 1)
    chan_t = iota((COLS, 512), 0)
    home_t = (slot_t // 8) * 4 + lax.rem(slot_t, 8)
    take_a = one_hot((home_t == chan_t) & (lax.rem(slot_t, 8) < 4))
    take_b = one_hot((home_t == chan_t + 4) & (lax.rem(slot_t, 8) >= 4))
    same = one_hot(iota((ROWS, ROWS), 0) == iota((ROWS, ROWS), 1))
    long_out = across(flip, plain(take_a, got).astype(BF))
    grad_gated = across(same, plain(take_b, got).astype(BF))
    y_all = so[0] * long_out
    y_hi = y_all.astype(BF)
    y_lo = (y_all - y_hi.astype(F32)).astype(BF)
    y_hi_t = across(same, y_hi).astype(BF)
    y_lo_t = across(same, y_lo).astype(BF)
    for i in range(TP):
        part[:, 256 * i : 256 * i + 256] = plain(y_hi_t, cot_all[i]) + plain(y_lo_t, cot_all[i])
    off = pl.multiple_of(other * HALF, HALF)
    mine = pl.multiple_of(dp * HALF, HALF)
    pair_out[...] = part[pl.ds(off, HALF), :].astype(BF)
    pair_copy = copy(pair_out, pair_in, 4, {"dp": other})
    pair_copy.start()
    for i in range(TP):
        mix_out[i] = (plain(y_hi, w_ref[:, 256 * i : 256 * i + 256]) + plain(y_lo, w_ref[:, 256 * i : 256 * i + 256])).astype(BF)
    mix_copies = []
    for k in range(1, TP):
        c = copy(mix_out.at[peer_tp(k)], mix_in.at[tp], 4 + k, {"tp": peer_tp(k)})
        c.start()
        mix_copies.append(c)

    def rows16(k):
        return pl.ds(pl.multiple_of(k * 16, 16), 16)

    def cols_of(k):
        return pl.ds(pl.multiple_of(k * HALF, HALF), HALF)

    pair_copy.wait()
    s1[...] = (part[pl.ds(mine, HALF), :] + pair_in[...].astype(F32)).astype(BF)
    first_copies = []
    for k in range(1, 8):
        c = copy(s1.at[rows16(peer1(k)), :], b1_in.at[k], 7 + k, dev1(k))
        c.start()
        first_copies.append(c)

    gso = [gy[...] * long_out, grad_gated * so[2], grad_gated * so[1]]
    edge_out[6:8, :] = jnp.zeros((2, COLS), F32)
    sm0[0, 9:16, :] = jnp.zeros((7, COLS), F32)
    for i in range(3):
        z1 = gso[i] * masks[0]
        z2 = gso[i] * masks[1]
        f0, f1, f2 = (taps_ref[i, s : s + 1, :] for s in range(TAPS))
        edge_out[2 * i : 2 * i + 1, :] = f2 * z2[0:1]
        edge_out[2 * i + 1 : 2 * i + 2, :] = f1 * z1[0:1] + f2 * z2[1:2]
        zbuf[0, 0:ROWS, :] = z1
        zbuf[1, 0:ROWS, :] = z2
        zbuf[:, ROWS : ROWS + 8, :] = jnp.zeros((2, 8, COLS), F32)
        sm0[0, 3 * i : 3 * i + 1, :] = jnp.sum(gso[i] * xe[i, 8 : 8 + ROWS, :], axis=0, keepdims=True)
        sm0[0, 3 * i + 1 : 3 * i + 2, :] = jnp.sum(z1 * xe[i, 7 : 7 + ROWS, :], axis=0, keepdims=True)
        sm0[0, 3 * i + 2 : 3 * i + 3, :] = jnp.sum(z2 * xe[i, 6 : 6 + ROWS, :], axis=0, keepdims=True)
        xe[i, 0:ROWS, :] = f0 * gso[i] + f1 * zbuf[0, 1 : 1 + ROWS, :] + f2 * zbuf[1, 2 : 2 + ROWS, :]
    edge_copy = copy(edge_out, edge_in, 15, {"ctx": peer_ctx(CTX - 1)})
    edge_copy.start()
    small_pair = copy(sm0.at[0], sm0.at[1], 16, {"dp": other})
    small_pair.start()

    for c in first_copies:
        c.wait()
    total = s1[rows16(my1), :].astype(F32)
    for k in range(1, 8):
        total += b1_in[k].astype(F32)
    s2[...] = total
    second_copies = []
    for k in range(1, 8):
        c = copy(s2.at[:, cols_of(peer2(k))], b2_in.at[k], 16 + k, dev2(k))
        c.start()
        second_copies.append(c)
    small_pair.wait()
    sm1[0] = sm0[0] + sm0[1]
    small_first = []
    for k in range(1, 8):
        c = copy(sm1.at[0], sm1.at[k], 23 + k, dev1(k))
        c.start()
        small_first.append(c)

    wait_all(lag_in, 3, all_rcv)
    for g in range(16):
        for h in range(2):
            value = lag_in[4 * g, h] + lag_in[4 * g + 1, h] + lag_in[4 * g + 2, h] + lag_in[4 * g + 3, h]
            lag_pair[0, g : g + 1, HALF * h : HALF * h + HALF] = value
    lag_copy = copy(lag_pair.at[0], lag_pair.at[1], 31, {"dp": other})
    lag_copy.start()

    for c in second_copies:
        c.wait()
    total = s2[:, cols_of(my2)]
    for k in range(1, 8):
        total += b2_in[k]
    g2[:, cols_of(my2)] = (total * scale).astype(BF)
    third_copies = []
    for k in range(1, 8):
        c = copy(g2.at[:, cols_of(my2)], g2.at[:, cols_of(my2)], 31 + k, dev2(k))
        c.start()
        third_copies.append(c)
    for c in small_first:
        c.wait()
    small = sm1[0]
    for k in range(1, 8):
        small += sm1[k]
    sm2[0] = small
    small_second = []
    for k in range(1, 8):
        c = copy(sm2.at[0], sm2.at[k], 38 + k, dev2(k))
        c.start()
        small_second.append(c)
    edge_copy.wait()
    for i in range(3):
        xe[i, ROWS - 2 : ROWS, :] += edge_in[2 * i : 2 * i + 2, :]
        gin_ref[i] = xe[i, 0:ROWS, :].astype(BF)

    for c in third_copies:
        c.wait()
    g1[rows16(my1), :] = g2[...]
    fourth_copies = []
    for k in range(1, 8):
        c = copy(g1.at[rows16(my1), :], g1.at[rows16(my1), :], 45 + k, dev1(k))
        c.start()
        fourth_copies.append(c)
    for c in mix_copies:
        c.wait()
    total = mix_out[pl.ds(tp, 1)].astype(F32)
    for k in range(1, TP):
        total += mix_in[pl.ds(peer_tp(k), 1)].astype(F32)
    mixed_ref[...] = total.reshape(ROWS, COLS).astype(BF)
    lag_copy.wait()
    glong_ref[...] = (lag_pair[0] + lag_pair[1]) * scale
    for c in small_second:
        c.wait()
    small = sm2[0]
    for k in range(1, 8):
        small += sm2[k]
    gtaps_ref[...] = small * scale
    for n in range(3):
        buf = (filt_in, send, ret)[n]
        wait_all(buf, n, all_snd)
    pltpu.make_async_copy(lag_in.at[pl.ds(0, CTX - 1)], lag_in.at[pl.ds(0, CTX - 1)], all_snd.at[3]).wait()
    for c in fourth_copies:
        c.wait()
    last_copy = copy(g1, gp, 53, {"dp": other})
    last_copy.start()
    gproj_ref[pl.ds(mine, HALF), :] = g1[...]
    last_copy.wait()
    gproj_ref[pl.ds(off, HALF), :] = gp[...]


def per_device(projected, segment_ids, short_filter, long_filter, out_proj, mixed_cotangent):
    scale = 1.0 / math.sqrt(2 * ROWS * CTX)
    V = pltpu.VMEM
    spec = pl.BlockSpec(memory_space=pltpu.VMEM)
    mixed, grad_in, grad_taps, grad_long, grad_proj = pl.pallas_call(
        functools.partial(layer, scale),
        out_shape=(
            jax.ShapeDtypeStruct((ROWS, COLS), BF),
            jax.ShapeDtypeStruct((3, ROWS, COLS), BF),
            jax.ShapeDtypeStruct((16, COLS), F32),
            jax.ShapeDtypeStruct((16, COLS), F32),
            jax.ShapeDtypeStruct((256, 1024), BF),
        ),
        in_specs=[spec] * 6,
        out_specs=[spec] * 5,
        scratch_shapes=[
            V((TP, ROWS, COLS), BF), V((8, COLS), F32), V((8, COLS), F32),
            V((16, 1, COLS), F32), V((CTX, 1, COLS), F32),
            V((3, ROWS + 8, COLS), F32), V((3, ROWS, COLS), F32), V((2, ROWS, COLS), F32), V((ROWS, COLS), F32),
            V((CTX, 8, ROWS), BF), V((CTX, 8, ROWS), BF),
            V((64 * 256 + 256, 256), BF), V((512, 1024), BF), V((512, 256), F32),
            V((256, 256), BF), V((4, 512, 256), BF), V((130, 1, HALF), F32), V((CTX, 2, 1, HALF), F32),
            V((CTX, 8, ROWS), BF), V((CTX, 8, ROWS), BF),
            V((2, ROWS + 8, COLS), F32), V((256, 1024), F32), V((TP, ROWS, COLS), BF), V((TP, ROWS, COLS), BF),
            V((HALF, 1024), BF), V((HALF, 1024), BF), V((HALF, 1024), BF), V((8, 16, 1024), BF),
            V((16, 1024), F32), V((8, 16, HALF), F32), V((16, 1024), BF), V((HALF, 1024), BF), V((HALF, 1024), BF),
            V((2, 16, COLS), F32), V((8, 16, COLS), F32), V((8, 16, COLS), F32),
            V((8, COLS), F32), V((8, COLS), F32), V((2, 16, COLS), F32),
            pltpu.SemaphoreType.DMA((54,)), pltpu.SemaphoreType.DMA((54,)),
            pltpu.SemaphoreType.DMA((4,)), pltpu.SemaphoreType.DMA((4,)),
        ],
        compiler_params=pltpu.CompilerParams(vmem_limit_bytes=48 << 20, collective_id=0, has_side_effects=True),
        name="layer",
    )(projected[:, 0], segment_ids, short_filter, long_filter, out_proj, mixed_cotangent[0])
    return (
        mixed[None],
        grad_in[:, None],
        grad_taps[:9].reshape(3, 3, COLS),
        grad_long,
        grad_proj.astype(F32),
    )


def solution(mesh):
    in_specs = (
        P(None, "dp", "ctx", "tp"),
        P("dp", "ctx"),
        P(None, None, "tp"),
        P("tp", "ctx"),
        P("tp", None),
        P("dp", "ctx", "tp"),
    )
    out_specs = (
        P("dp", "ctx", "tp"),
        P(None, "dp", "ctx", "tp"),
        P(None, None, "tp"),
        P("tp", "ctx"),
        P("tp", None),
    )
    return jax.shard_map(
        per_device, mesh=mesh, in_specs=in_specs, out_specs=out_specs, check_vma=False
    )
```

```python
import functools
import math

import jax
import jax.numpy as jnp
from jax import lax
from jax.experimental import pallas as pl
from jax.experimental.pallas import tpu as pltpu
from jax.sharding import PartitionSpec as P

F32 = jnp.float32
BF = jnp.bfloat16
MESH = pl.DeviceIdType.MESH
CTX = 64
TP = 4
TAPS = 3
ROWS = 256
COLS = 256
HALF = 128


def iota(shape, axis):
    return lax.broadcasted_iota(jnp.int32, shape, axis)


def one_hot(condition):
    return jnp.where(condition, 1.0, 0.0).astype(BF)


def across(a, b):
    return lax.dot_general(a, b, (((1,), (1,)), ((), ())), preferred_element_type=F32)


def plain(a, b):
    return jnp.dot(a, b, preferred_element_type=F32)


def layer(
    scale,
    x_hbm, seg_hbm, taps_hbm, filt_hbm, w_hbm, cot_hbm,
    mixed_ref, gin_ref, gtaps_ref, glong_ref, gproj_ref,
    x_ref, seg_ref, taps_ref, filt_ref, w_ref, load_sem,
    cot_all, halo_out, halo_in, filt_out, filt_in, xe, so, masks, gy,
    send_g, recv_g, send_l, recv_l, toep, stacked, acc, gct, gls, kept, lag_out, lag_in,
    ret_f, back_f, ret_b, back_b, zbuf, y_t, part, mix_out, mix_in,
    pair_out, pair_in, sum_out, sum_in, one_tile, tiles, tiles_in,
    sm0, sm1, sm2, edge_out, edge_in, lag_pair,
    snd, rcv, all_snd, all_rcv, grp,
):
    ctx = lax.axis_index("ctx")
    tp = lax.axis_index("tp")
    dp = lax.axis_index("dp")
    y = lax.rem(ctx, 8)
    z = ctx // 8
    my1 = y * (1 - dp) + z * dp
    my2 = z * (1 - dp) + y * dp
    step1 = 1 + 7 * dp
    step2 = 8 - 7 * dp
    base1 = ctx - my1 * step1
    base2 = ctx - my2 * step2
    other = 1 - dp

    def peer1(k):
        return lax.rem(my1 + k, 8)

    def dev1(k):
        return {"ctx": base1 + peer1(k) * step1}

    def peer2(k):
        return lax.rem(my2 + k, 8)

    def dev2(k):
        return {"ctx": base2 + peer2(k) * step2}

    def peer_tp(k):
        return lax.rem(tp + k, TP)

    def peer_ctx(k):
        return lax.rem(ctx + k, CTX)

    def copy(src, dst, n, dev):
        return pltpu.make_async_remote_copy(
            src, dst, snd.at[n], rcv.at[n], device_id=dev, device_id_type=MESH
        )

    barrier = pltpu.get_barrier_semaphore()

    def greet(k, carry):
        pl.semaphore_signal(barrier, 1, device_id={"ctx": peer_ctx(k)}, device_id_type=MESH)
        return carry

    for k in range(1, TP):
        pl.semaphore_signal(barrier, 1, device_id={"tp": peer_tp(k)}, device_id_type=MESH)
    pl.semaphore_signal(barrier, 1, device_id={"dp": other}, device_id_type=MESH)
    lax.fori_loop(1, CTX, greet, 0)
    loads = []
    for n, (src, dst) in enumerate((
        (filt_hbm, filt_ref), (seg_hbm, seg_ref), (x_hbm, x_ref),
        (cot_hbm, cot_all.at[tp]), (taps_hbm, taps_ref), (w_hbm, w_ref),
    )):
        load = pltpu.make_async_copy(src, dst, load_sem.at[n])
        load.start()
        loads.append(load)

    for load in loads[:3]:
        load.wait()
    rows128 = iota((HALF, HALF), 0)
    cols128 = iota((HALF, HALF), 1)
    flip128 = one_hot(rows128 + cols128 == HALF - 1)
    filt = filt_ref[...].astype(BF)
    filt_out[...] = jnp.concatenate(
        [plain(filt[:, :HALF], flip128), plain(filt[:, HALF:], flip128)], axis=1
    ).reshape(16, 1, COLS)
    seg_row = seg_ref[...].astype(F32)
    seg_col = jnp.transpose(jnp.broadcast_to(seg_row, (HALF, ROWS)))
    halo_out[0:6, :] = jnp.concatenate([x_ref[i, ROWS - 2 : ROWS, :].astype(F32) for i in range(3)], axis=0)
    halo_out[6:8, :] = jnp.concatenate([seg_col[ROWS - 2 : ROWS, :]] * 2, axis=1)
    loads[3].wait()
    pl.semaphore_wait(barrier, CTX - 1 + TP - 1 + 1)

    halo = copy(halo_out, halo_in, 0, {"ctx": peer_ctx(1)})
    halo.start()
    cot_copies = []
    for k in range(1, TP):
        c = copy(cot_all.at[tp], cot_all.at[tp], k, {"tp": peer_tp(k)})
        c.start()
        cot_copies.append(c)

    def send_filter(k, carry):
        peer = peer_ctx(k)
        pltpu.make_async_remote_copy(
            filt_out.at[peer // 4], filt_in.at[ctx], all_snd.at[0], all_rcv.at[0],
            device_id={"ctx": peer}, device_id_type=MESH,
        ).start()
        return carry

    lax.fori_loop(1, CTX, send_filter, 0)
    filt_in[pl.ds(ctx, 1)] = filt_out[pl.ds(ctx // 4, 1)]

    def wait_all(buf, n, which):
        pltpu.make_async_copy(buf.at[pl.ds(0, CTX - 1)], buf.at[pl.ds(0, CTX - 1)], which.at[n]).wait()

    for i in range(3):
        xe[i, 8 : 8 + ROWS, :] = x_ref[i].astype(F32)
    halo.wait()
    loads[4].wait()
    loads[5].wait()

    for i in range(3):
        xe[i, 6:8, :] = halo_in[2 * i : 2 * i + 2, :]
    prev_seg = jnp.where(ctx == 0, -1.0, halo_in[6:8, 0:HALF])
    before1 = jnp.concatenate([prev_seg[1:2], seg_col[: ROWS - 1]], axis=0)
    before2 = jnp.concatenate([prev_seg, seg_col[: ROWS - 2]], axis=0)
    for n, before in enumerate((before1, before2)):
        mask = jnp.where(before == seg_col, 1.0, 0.0)
        masks[n] = jnp.concatenate([mask, mask], axis=1)

    def featurize(i):
        so[i] = (
            taps_ref[i, 0:1, :] * xe[i, 8 : 8 + ROWS, :]
            + taps_ref[i, 1:2, :] * masks[0] * xe[i, 7 : 7 + ROWS, :]
            + taps_ref[i, 2:3, :] * masks[1] * xe[i, 6 : 6 + ROWS, :]
        )

    featurize(1)
    featurize(2)

    def scatter(src, dst, n):
        def one(k, carry):
            peer = peer_ctx(k)
            pltpu.make_async_remote_copy(
                src.at[peer], dst.at[ctx], all_snd.at[n], all_rcv.at[n],
                device_id={"ctx": peer}, device_id_type=MESH,
            ).start()
            return carry

        lax.fori_loop(1, CTX, one, 0)
        dst[pl.ds(ctx, 1)] = src[pl.ds(ctx, 1)]

    slot = iota((512, COLS), 0)
    chan = iota((512, COLS), 1)
    home = (slot // 8) * 4 + lax.rem(slot, 8)
    pick_a = one_hot((home == chan) & (lax.rem(slot, 8) < 4))
    pick_b = one_hot((home == chan + 4) & (lax.rem(slot, 8) >= 4))
    flip = one_hot(iota((ROWS, ROWS), 0) + iota((ROWS, ROWS), 1) == ROWS - 1)

    def tiles_of(value):
        return (across(pick_a, value[:HALF]) + across(pick_b, value[HALF:])).reshape(CTX, 8, HALF).astype(BF)

    send_g[...] = tiles_of(plain(flip, (so[1] * so[2]).astype(BF)).astype(BF))
    scatter(send_g, recv_g, 1)
    featurize(0)

    wait_all(filt_in, 0, all_rcv)
    keep = rows128 >= cols128

    def spread(line):
        return pltpu.roll(jnp.broadcast_to(line, (HALF, HALF)), 1, 1, stride=1, stride_axis=0)

    def build(n, prev):
        for u in range(2):
            d = 2 * n + u
            line = filt_in[d]
            s0 = spread(line[:, :HALF])
            a0 = jnp.where(keep, s0, prev).astype(BF)
            s1_ = spread(line[:, HALF:])
            a1 = jnp.where(keep, s1_, s0).astype(BF)
            base = pl.multiple_of(d * 256, 256)
            toep[pl.ds(base, HALF), 0:HALF] = a0
            toep[pl.ds(base + HALF, HALF), HALF:COLS] = a0
            toep[pl.ds(base + HALF, HALF), 0:HALF] = a1
            toep[pl.ds(base + 256, HALF), HALF:COLS] = a1
            prev = s1_
        return prev

    toep[0:HALF, HALF:COLS] = jnp.zeros((HALF, HALF), BF)
    lax.fori_loop(0, 32, build, jnp.zeros((HALF, HALF), F32))

    for c in cot_copies:
        c.wait()
    total = across(cot_all[0], w_ref[:, 0:256])
    for i in range(1, TP):
        total += across(cot_all[i], w_ref[:, 256 * i : 256 * i + 256])
    gy[...] = total
    send_l[...] = tiles_of((total * so[0]).astype(BF))
    scatter(send_l, recv_l, 2)

    first3 = iota((32, 8, HALF), 1) < 4

    def swap4(value):
        return pltpu.roll(value, 4, 1)

    def halves(ref):
        both = ref[...].astype(F32).reshape(32, 16, HALF)
        return both[:, 0:8], both[:, 8:16]

    def rows_of(one, two):
        return jnp.concatenate(
            [jnp.where(first3, one, swap4(two)), jnp.where(first3, swap4(one), two)], axis=2
        ).reshape(256, COLS)

    def backwards(value):
        return jnp.concatenate([value[31 - i : 32 - i] for i in range(32)], axis=0)

    def convolve(rows):
        for e in range(4):
            if e:
                stacked[:, 256 * e : 256 * e + 256] = jnp.concatenate(
                    [jnp.zeros((4 * e, COLS), F32), rows[: 256 - 4 * e]], axis=0
                ).astype(BF)
            else:
                stacked[:, 0:256] = rows.astype(BF)
        for n in range(16):
            term = plain(stacked[0 : 256 - 16 * n, :], toep[1024 * n : 1024 * n + 1024, :])
            if n:
                acc[16 * n : 256, :] += term
            else:
                acc[...] = term
        done = acc[...].reshape(32, 8, COLS)
        low = done[:, :, :HALF]
        high = done[:, :, HALF:]
        return jnp.where(first3, low, swap4(high)), jnp.where(first3, swap4(low), high)

    def give(ref, one, two):
        ref[...] = jnp.concatenate([one, two], axis=1).reshape(CTX, 8, HALF).astype(BF)

    wait_all(recv_g, 1, all_rcv)
    even, odd = halves(recv_g)
    rows_g = rows_of(even, odd)
    one, two = convolve(rows_g)
    give(ret_f, one, two)
    scatter(ret_f, back_f, 3)
    gct[...] = jnp.transpose(rows_g).astype(BF)

    wait_all(recv_l, 2, all_rcv)
    even, odd = halves(recv_l)
    one, two = convolve(rows_of(backwards(odd), backwards(even)))
    give(ret_b, backwards(two), backwards(one))
    scatter(ret_b, back_b, 4)

    straight = rows_of(even, odd)
    next_even = jnp.concatenate([even[1:], jnp.zeros((1, 8, HALF), F32)], axis=0)
    crossed = rows_of(odd, next_even)
    zero8 = jnp.zeros((8, COLS), F32)
    for n, value in enumerate(
        (straight, crossed, jnp.concatenate([straight[8:], zero8], axis=0), jnp.concatenate([crossed[8:], zero8], axis=0))
    ):
        gls[n, 0:256, :] = value.astype(BF)
        gls[n, 256:512, :] = jnp.zeros((256, COLS), BF)
    later = cols128 > rows128

    def roll_up(block):
        return pltpu.roll(block, 1, 1, stride=1, stride_axis=0)

    def lag_row(now, last):
        return jnp.sum(jnp.where(later, now, last), axis=0, keepdims=True).reshape(1, 1, HALF)

    def correlate(width):
        def body(m, carry):
            c11, last = carry
            for u in range(4):
                c = plain(gct[:, 0:width], gls[u, pl.ds(pl.multiple_of(16 * m, 16), width), :])
                r0 = roll_up(c11 + c[:HALF, :HALF])
                r1 = roll_up(c[:HALF, HALF:] + c[HALF:, :HALF])
                lag_out[pl.ds(8 * m + 2 * u, 1)] = lag_row(r0, last)
                lag_out[pl.ds(8 * m + 2 * u + 1, 1)] = lag_row(r1, r0)
                c11 = c[HALF:, HALF:]
                last = r1
            return c11, last

        return body

    nothing = jnp.zeros((HALF, HALF), F32)
    c11, last = lax.fori_loop(0, 6, correlate(256), (nothing, nothing))
    kept[0] = c11
    kept[1] = last

    slot_t = iota((COLS, 512), 1)
    chan_t = iota((COLS, 512), 0)
    home_t = (slot_t // 8) * 4 + lax.rem(slot_t, 8)
    take_a = one_hot((home_t == chan_t) & (lax.rem(slot_t, 8) < 4))
    take_b = one_hot((home_t == chan_t + 4) & (lax.rem(slot_t, 8) >= 4))
    same = one_hot(iota((ROWS, ROWS), 0) == iota((ROWS, ROWS), 1))

    def channels(ref):
        got = ref[...].astype(F32).reshape(512, HALF).astype(BF)
        return jnp.concatenate([plain(take_a, got), plain(take_b, got)], axis=1).astype(BF)

    wait_all(back_f, 3, all_rcv)
    long_out = across(flip, channels(back_f))
    y_all = so[0] * long_out
    y_hi = y_all.astype(BF)
    y_lo = (y_all - y_hi.astype(F32)).astype(BF)
    y_t[0] = across(same, y_hi).astype(BF)
    y_t[1] = across(same, y_lo).astype(BF)
    off = pl.multiple_of(other * HALF, HALF)
    mine = pl.multiple_of(dp * HALF, HALF)
    pair_copies = []
    for i in range(TP):
        pair_out[i] = (
            plain(y_t[0, pl.ds(off, HALF), :], cot_all[i]) + plain(y_t[1, pl.ds(off, HALF), :], cot_all[i])
        ).astype(BF)
        c = copy(pair_out.at[i], pair_in.at[i], 8 + i, {"dp": other})
        c.start()
        pair_copies.append(c)
    for i in range(TP):
        part[:, 256 * i : 256 * i + 256] = plain(y_t[0, pl.ds(mine, HALF), :], cot_all[i]) + plain(
            y_t[1, pl.ds(mine, HALF), :], cot_all[i]
        )
    mix_copies = []
    for i in range(TP):
        mix_out[i] = (
            plain(y_hi, w_ref[:, 256 * i : 256 * i + 256]) + plain(y_lo, w_ref[:, 256 * i : 256 * i + 256])
        ).astype(BF)
    for k in range(1, TP):
        c = copy(mix_out.at[peer_tp(k)], mix_in.at[tp], 4 + k, {"tp": peer_tp(k)})
        c.start()
        mix_copies.append(c)

    for i in range(TP):
        pair_copies[i].wait()
        both = part[:, 256 * i : 256 * i + 256] + pair_in[i].astype(F32)
        for r in range(8):
            for h in range(2):
                sum_out[8 * r + 2 * i + h] = both[16 * r : 16 * r + 16, HALF * h : HALF * h + HALF].astype(BF)
    scatter(sum_out, sum_in, 6)

    c11, last = lax.fori_loop(6, 8, correlate(256), (kept[0], kept[1]))
    c11, last = lax.fori_loop(8, 16, correlate(128), (c11, last))
    r0 = roll_up(c11)
    lag_out[128:129] = lag_row(r0, last)
    lag_out[129:130] = lag_row(nothing, r0)

    def send_lags(k, carry):
        peer = peer_ctx(k)
        pltpu.make_async_remote_copy(
            lag_out.at[pl.ds(2 * peer + 2, 2)], lag_in.at[ctx], all_snd.at[5], all_rcv.at[5],
            device_id={"ctx": peer}, device_id_type=MESH,
        ).start()
        return carry

    lax.fori_loop(1, CTX, send_lags, 0)
    lag_in[pl.ds(ctx, 1)] = lag_out[pl.ds(2 * ctx + 2, 2)].reshape(1, 2, 1, HALF)

    wait_all(back_b, 4, all_rcv)
    grad_gated = across(same, channels(back_b))
    edge_out[6:8, :] = jnp.zeros((2, COLS), F32)
    sm0[0, 9:16, :] = jnp.zeros((7, COLS), F32)
    for i in range(3):
        gso = (gy[...] * long_out, grad_gated * so[2], grad_gated * so[1])[i]
        z1 = gso * masks[0]
        z2 = gso * masks[1]
        f0, f1, f2 = (taps_ref[i, s : s + 1, :] for s in range(TAPS))
        edge_out[2 * i : 2 * i + 1, :] = f2 * z2[0:1]
        edge_out[2 * i + 1 : 2 * i + 2, :] = f1 * z1[0:1] + f2 * z2[1:2]
        zbuf[0, 0:ROWS, :] = z1
        zbuf[1, 0:ROWS, :] = z2
        zbuf[:, ROWS : ROWS + 8, :] = jnp.zeros((2, 8, COLS), F32)
        sm0[0, 3 * i : 3 * i + 1, :] = jnp.sum(gso * xe[i, 8 : 8 + ROWS, :], axis=0, keepdims=True)
        sm0[0, 3 * i + 1 : 3 * i + 2, :] = jnp.sum(z1 * xe[i, 7 : 7 + ROWS, :], axis=0, keepdims=True)
        sm0[0, 3 * i + 2 : 3 * i + 3, :] = jnp.sum(z2 * xe[i, 6 : 6 + ROWS, :], axis=0, keepdims=True)
        xe[i, 0:ROWS, :] = f0 * gso + f1 * zbuf[0, 1 : 1 + ROWS, :] + f2 * zbuf[1, 2 : 2 + ROWS, :]
    edge_copy = copy(edge_out, edge_in, 15, {"ctx": peer_ctx(CTX - 1)})
    edge_copy.start()
    small_pair = copy(sm0.at[0], sm0.at[1], 16, {"dp": other})
    small_pair.start()

    wait_all(sum_in, 6, all_rcv)
    total = sum_in[0].astype(F32)
    for n in range(1, CTX):
        total += sum_in[n].astype(F32)
    one_tile[...] = (total * scale).astype(BF)

    def share(k, carry):
        pltpu.make_async_remote_copy(
            one_tile, tiles.at[ctx], all_snd.at[7], grp.at[ctx // 16],
            device_id={"ctx": peer_ctx(k)}, device_id_type=MESH,
        ).start()
        return carry

    lax.fori_loop(1, CTX, share, 0)
    pltpu.make_async_copy(one_tile, tiles.at[ctx], grp.at[ctx // 16]).start()

    small_pair.wait()
    sm1[0] = sm0[0] + sm0[1]
    small_first = []
    for k in range(1, 8):
        c = copy(sm1.at[0], sm1.at[k], 23 + k, dev1(k))
        c.start()
        small_first.append(c)
    edge_copy.wait()
    for i in range(3):
        xe[i, ROWS - 2 : ROWS, :] += edge_in[2 * i : 2 * i + 2, :]
        gin_ref[i] = xe[i, 0:ROWS, :].astype(BF)
    for c in mix_copies:
        c.wait()
    total = mix_out[pl.ds(tp, 1)].astype(F32)
    for k in range(1, TP):
        total += mix_in[pl.ds(peer_tp(k), 1)].astype(F32)
    mixed_ref[...] = total.reshape(ROWS, COLS).astype(BF)
    for c in small_first:
        c.wait()
    small = sm1[0]
    for k in range(1, 8):
        small += sm1[k]
    sm2[0] = small
    small_second = []
    for k in range(1, 8):
        c = copy(sm2.at[0], sm2.at[k], 38 + k, dev2(k))
        c.start()
        small_second.append(c)

    wait_all(lag_in, 5, all_rcv)
    for g in range(16):
        for h in range(2):
            value = lag_in[4 * g, h] + lag_in[4 * g + 1, h] + lag_in[4 * g + 2, h] + lag_in[4 * g + 3, h]
            lag_pair[0, g : g + 1, HALF * h : HALF * h + HALF] = value
    lag_copy = copy(lag_pair.at[0], lag_pair.at[1], 31, {"dp": other})
    lag_copy.start()

    last_copies = []
    for q in range(4):
        group = pl.ds(16 * q, 16)
        pltpu.make_async_copy(tiles.at[group], tiles.at[group], grp.at[q]).wait()
        c = copy(tiles.at[group], tiles_in.at[group], 17 + q, {"dp": other})
        c.start()
        last_copies.append(c)
    for q in range(CTX):
        gproj_ref[pl.ds(pl.multiple_of(mine + 16 * (q // 8), 16), 16), HALF * (q % 8) : HALF * (q % 8) + HALF] = tiles[q]
    lag_copy.wait()
    glong_ref[...] = (lag_pair[0] + lag_pair[1]) * scale
    for c in small_second:
        c.wait()
    small = sm2[0]
    for k in range(1, 8):
        small += sm2[k]
    small = small * scale
    for i in range(3):
        gtaps_ref[i] = small[3 * i : 3 * i + 3, :]
    for n, buf in enumerate((filt_in, send_g, send_l, ret_f, ret_b, lag_in, sum_in, tiles)):
        wait_all(buf, n, all_snd)
    for c in last_copies:
        c.wait()
    for q in range(CTX):
        gproj_ref[pl.ds(pl.multiple_of(off + 16 * (q // 8), 16), 16), HALF * (q % 8) : HALF * (q % 8) + HALF] = tiles_in[q]


def store(mixed, gin, gtaps, glong, gproj, mixed_o, gin_o, gtaps_o, glong_o, gproj_o, wide, sem):
    copies = []
    for n, (src, dst) in enumerate(((gin, gin_o), (mixed, mixed_o), (glong, glong_o), (gtaps, gtaps_o))):
        c = pltpu.make_async_copy(src, dst, sem.at[n])
        c.start()
        copies.append(c)
    for n in range(2):
        rows = pl.ds(HALF * n, HALF)
        wide[rows, :] = gproj[rows, :].astype(F32)
        c = pltpu.make_async_copy(wide.at[rows, :], gproj_o.at[rows, :], sem.at[4 + n])
        c.start()
        copies.append(c)
    for c in copies:
        c.wait()


def per_device(projected, segment_ids, short_filter, long_filter, out_proj, mixed_cotangent):
    scale = 1.0 / math.sqrt(2 * ROWS * CTX)
    V = pltpu.VMEM
    spec = pl.BlockSpec(memory_space=pltpu.VMEM)
    mixed, grad_in, grad_taps, grad_long, grad_proj = pl.pallas_call(
        functools.partial(layer, scale),
        out_shape=(
            jax.ShapeDtypeStruct((ROWS, COLS), BF),
            jax.ShapeDtypeStruct((3, ROWS, COLS), BF),
            jax.ShapeDtypeStruct((3, TAPS, COLS), F32),
            jax.ShapeDtypeStruct((16, COLS), F32),
            jax.ShapeDtypeStruct((256, 1024), BF),
        ),
        in_specs=[pl.BlockSpec(memory_space=pltpu.HBM)] * 6,
        out_specs=[spec] * 5,
        scratch_shapes=[
            V((3, ROWS, COLS), BF), V((1, ROWS), jnp.int32), V((3, TAPS, COLS), F32), V((16, COLS), F32), V((256, 1024), BF),
            pltpu.SemaphoreType.DMA((6,)),
            V((TP, ROWS, COLS), BF), V((8, COLS), F32), V((8, COLS), F32),
            V((16, 1, COLS), F32), V((CTX, 1, COLS), F32),
            V((3, ROWS + 8, COLS), F32), V((3, ROWS, COLS), F32), V((2, ROWS, COLS), F32), V((ROWS, COLS), F32),
            V((CTX, 8, HALF), BF), V((CTX, 8, HALF), BF), V((CTX, 8, HALF), BF), V((CTX, 8, HALF), BF),
            V((64 * 256 + 256, 256), BF), V((256, 1024), BF), V((256, 256), F32),
            V((256, 256), BF), V((4, 512, 256), BF), V((2, HALF, HALF), F32), V((130, 1, HALF), F32), V((CTX, 2, 1, HALF), F32),
            V((CTX, 8, HALF), BF), V((CTX, 8, HALF), BF), V((CTX, 8, HALF), BF), V((CTX, 8, HALF), BF),
            V((2, ROWS + 8, COLS), F32), V((2, COLS, ROWS), BF), V((HALF, 1024), F32),
            V((TP, ROWS, COLS), BF), V((TP, ROWS, COLS), BF),
            V((TP, HALF, COLS), BF), V((TP, HALF, COLS), BF),
            V((CTX, 16, HALF), BF), V((CTX, 16, HALF), BF), V((16, HALF), BF), V((CTX, 16, HALF), BF), V((CTX, 16, HALF), BF),
            V((2, 16, COLS), F32), V((8, 16, COLS), F32), V((8, 16, COLS), F32),
            V((8, COLS), F32), V((8, COLS), F32), V((2, 16, COLS), F32),
            pltpu.SemaphoreType.DMA((46,)), pltpu.SemaphoreType.DMA((46,)),
            pltpu.SemaphoreType.DMA((8,)), pltpu.SemaphoreType.DMA((8,)), pltpu.SemaphoreType.DMA((4,)),
        ],
        compiler_params=pltpu.CompilerParams(vmem_limit_bytes=48 << 20, collective_id=0, has_side_effects=True),
        name="layer",
    )(*(pltpu.with_memory_space_constraint(v, pltpu.HBM) for v in (projected[:, 0], segment_ids, short_filter, long_filter, out_proj, mixed_cotangent[0])))
    mixed, grad_in, grad_taps, grad_long, grad_proj = pl.pallas_call(
        store,
        out_shape=(
            jax.ShapeDtypeStruct((ROWS, COLS), BF),
            jax.ShapeDtypeStruct((3, ROWS, COLS), BF),
            jax.ShapeDtypeStruct((3, TAPS, COLS), F32),
            jax.ShapeDtypeStruct((16, COLS), F32),
            jax.ShapeDtypeStruct((256, 1024), F32),
        ),
        in_specs=[spec] * 5,
        out_specs=[pl.BlockSpec(memory_space=pltpu.HBM)] * 5,
        scratch_shapes=[V((256, 1024), F32), pltpu.SemaphoreType.DMA((6,))],
        compiler_params=pltpu.CompilerParams(vmem_limit_bytes=8 << 20),
        name="store",
    )(mixed, grad_in, grad_taps, grad_long, grad_proj)
    return (mixed[None], grad_in[:, None], grad_taps, grad_long, grad_proj)


def solution(mesh):
    in_specs = (
        P(None, "dp", "ctx", "tp"),
        P("dp", "ctx"),
        P(None, None, "tp"),
        P("tp", "ctx"),
        P("tp", None),
        P("dp", "ctx", "tp"),
    )
    out_specs = (
        P("dp", "ctx", "tp"),
        P(None, "dp", "ctx", "tp"),
        P(None, None, "tp"),
        P("tp", "ctx"),
        P("tp", None),
    )
    return jax.shard_map(
        per_device, mesh=mesh, in_specs=in_specs, out_specs=out_specs, check_vma=False
    )
```

```python
import functools
import math

import jax
import jax.numpy as jnp
from jax import lax
from jax.experimental import pallas as pl
from jax.experimental.pallas import tpu as pltpu
from jax.sharding import PartitionSpec as P

F32 = jnp.float32
BF = jnp.bfloat16
MESH = pl.DeviceIdType.MESH
CTX = 64
TP = 4
TAPS = 3
ROWS = 256
COLS = 256
HALF = 128


def iota(shape, axis):
    return lax.broadcasted_iota(jnp.int32, shape, axis)


def one_hot(condition):
    return jnp.where(condition, 1.0, 0.0).astype(BF)


def across(a, b):
    return lax.dot_general(a, b, (((1,), (1,)), ((), ())), preferred_element_type=F32)


def plain(a, b):
    return jnp.dot(a, b, preferred_element_type=F32)


def layer(
    scale,
    x_hbm, seg_hbm, taps_hbm, filt_hbm, w_hbm, cot_hbm,
    mixed_ref, gin_ref, gtaps_ref, glong_ref, gproj_ref,
    x_ref, seg_ref, taps_ref, filt_ref, w_ref, load_sem, picks, flips,
    cot_all, halo_out, halo_in, filt_out, filt_in, xe, so, masks, gy,
    send_g, recv_g, send_l, recv_l, toep, stacked, acc, gct, gls, lag_out, lag_in,
    ret_f, back_f, ret_b, back_b, zbuf, y_t, part, mix_out, mix_in,
    pair_out, pair_in, sum_out, sum_in, one_tile, tiles, tiles_in,
    sm0, sm1, sm2, edge_out, edge_in, lag_pair,
    snd, rcv, all_snd, all_rcv, grp,
):
    ctx = lax.axis_index("ctx")
    tp = lax.axis_index("tp")
    dp = lax.axis_index("dp")
    y = lax.rem(ctx, 8)
    z = ctx // 8
    my1 = y * (1 - dp) + z * dp
    my2 = z * (1 - dp) + y * dp
    step1 = 1 + 7 * dp
    step2 = 8 - 7 * dp
    base1 = ctx - my1 * step1
    base2 = ctx - my2 * step2
    other = 1 - dp

    def peer1(k):
        return lax.rem(my1 + k, 8)

    def dev1(k):
        return {"ctx": base1 + peer1(k) * step1}

    def peer2(k):
        return lax.rem(my2 + k, 8)

    def dev2(k):
        return {"ctx": base2 + peer2(k) * step2}

    def peer_tp(k):
        return lax.rem(tp + k, TP)

    def peer_ctx(k):
        return lax.rem(ctx + k, CTX)

    def reach(k):
        half = (k + 1) // 2
        return 4 + half * (2 * lax.rem(k + 1, 2) - 1)

    def peer_far(k):
        return lax.rem(z + reach(k // 8), 8) * 8 + lax.rem(y + reach(lax.rem(k, 8)), 8)

    def copy(src, dst, n, dev):
        return pltpu.make_async_remote_copy(
            src, dst, snd.at[n], rcv.at[n], device_id=dev, device_id_type=MESH
        )

    barrier = pltpu.get_barrier_semaphore()

    def greet(k, carry):
        pl.semaphore_signal(barrier, 1, device_id={"ctx": peer_far(k)}, device_id_type=MESH)
        return carry

    for k in range(1, TP):
        pl.semaphore_signal(barrier, 1, device_id={"tp": peer_tp(k)}, device_id_type=MESH)
    pl.semaphore_signal(barrier, 1, device_id={"dp": other}, device_id_type=MESH)
    lax.fori_loop(0, CTX - 1, greet, 0)
    loads = []
    for n, (src, dst) in enumerate((
        (filt_hbm, filt_ref), (seg_hbm, seg_ref), (x_hbm, x_ref),
        (cot_hbm, cot_all.at[tp]), (taps_hbm, taps_ref), (w_hbm, w_ref),
    )):
        load = pltpu.make_async_copy(src, dst, load_sem.at[n])
        load.start()
        loads.append(load)

    for load in loads[:3]:
        load.wait()
    rows128 = iota((HALF, HALF), 0)
    cols128 = iota((HALF, HALF), 1)
    flip128 = one_hot(rows128 + cols128 == HALF - 1)
    filt = filt_ref[...].astype(BF)
    filt_out[...] = jnp.concatenate(
        [plain(filt[:, :HALF], flip128), plain(filt[:, HALF:], flip128)], axis=1
    ).reshape(16, 1, COLS)
    seg_row = seg_ref[...].astype(F32)
    seg_col = jnp.transpose(jnp.broadcast_to(seg_row, (HALF, ROWS)))
    halo_out[0:6, :] = jnp.concatenate([x_ref[i, ROWS - 2 : ROWS, :].astype(F32) for i in range(3)], axis=0)
    halo_out[6:8, :] = jnp.concatenate([seg_col[ROWS - 2 : ROWS, :]] * 2, axis=1)
    slot = iota((512, COLS), 0)
    chan = iota((512, COLS), 1)
    home = (slot // 8) * 4 + lax.rem(slot, 8)
    picks[0] = one_hot((home == chan) & (lax.rem(slot, 8) < 4))
    picks[1] = one_hot((home == chan + 4) & (lax.rem(slot, 8) >= 4))
    flips[0] = one_hot(iota((ROWS, ROWS), 0) + iota((ROWS, ROWS), 1) == ROWS - 1)
    flips[1] = one_hot(iota((ROWS, ROWS), 0) == iota((ROWS, ROWS), 1))
    for i in range(3):
        xe[i, 8 : 8 + ROWS, :] = x_ref[i].astype(F32)
    loads[3].wait()
    pl.semaphore_wait(barrier, CTX - 1 + TP - 1 + 1)

    halo = copy(halo_out, halo_in, 0, {"ctx": peer_ctx(1)})
    halo.start()
    cot_copies = []
    for k in range(1, TP):
        c = copy(cot_all.at[tp], cot_all.at[tp], k, {"tp": peer_tp(k)})
        c.start()
        cot_copies.append(c)

    def send_filter(k, carry):
        peer = peer_far(k)
        pltpu.make_async_remote_copy(
            filt_out.at[peer // 4], filt_in.at[ctx], all_snd.at[0], all_rcv.at[0],
            device_id={"ctx": peer}, device_id_type=MESH,
        ).start()
        return carry

    lax.fori_loop(0, CTX - 1, send_filter, 0)
    filt_in[pl.ds(ctx, 1)] = filt_out[pl.ds(ctx // 4, 1)]

    def wait_all(buf, n, which):
        pltpu.make_async_copy(buf.at[pl.ds(0, CTX - 1)], buf.at[pl.ds(0, CTX - 1)], which.at[n]).wait()

    halo.wait()
    loads[4].wait()
    loads[5].wait()

    for i in range(3):
        xe[i, 6:8, :] = halo_in[2 * i : 2 * i + 2, :]
    prev_seg = jnp.where(ctx == 0, -1.0, halo_in[6:8, 0:HALF])
    before1 = jnp.concatenate([prev_seg[1:2], seg_col[: ROWS - 1]], axis=0)
    before2 = jnp.concatenate([prev_seg, seg_col[: ROWS - 2]], axis=0)
    for n, before in enumerate((before1, before2)):
        mask = jnp.where(before == seg_col, 1.0, 0.0)
        masks[n] = jnp.concatenate([mask, mask], axis=1)

    def featurize(i):
        so[i] = (
            taps_ref[i, 0:1, :] * xe[i, 8 : 8 + ROWS, :]
            + taps_ref[i, 1:2, :] * masks[0] * xe[i, 7 : 7 + ROWS, :]
            + taps_ref[i, 2:3, :] * masks[1] * xe[i, 6 : 6 + ROWS, :]
        )

    featurize(1)
    featurize(2)

    def scatter(src, dst, n):
        def one(k, carry):
            peer = peer_far(k)
            pltpu.make_async_remote_copy(
                src.at[peer], dst.at[ctx], all_snd.at[n], all_rcv.at[n],
                device_id={"ctx": peer}, device_id_type=MESH,
            ).start()
            return carry

        lax.fori_loop(0, CTX - 1, one, 0)
        dst[pl.ds(ctx, 1)] = src[pl.ds(ctx, 1)]

    def tiles_of(value):
        return (across(picks[0], value[:HALF]) + across(picks[1], value[HALF:])).reshape(CTX, 8, HALF).astype(BF)

    send_g[...] = tiles_of(plain(flips[0], (so[1] * so[2]).astype(BF)).astype(BF))
    scatter(send_g, recv_g, 1)
    featurize(0)

    wait_all(filt_in, 0, all_rcv)
    keep = rows128 >= cols128

    def spread(line):
        return pltpu.roll(jnp.broadcast_to(line, (HALF, HALF)), 1, 1, stride=1, stride_axis=0)

    def build(n, prev):
        for u in range(2):
            d = 2 * n + u
            line = filt_in[d]
            s0 = spread(line[:, :HALF])
            a0 = jnp.where(keep, s0, prev).astype(BF)
            s1_ = spread(line[:, HALF:])
            a1 = jnp.where(keep, s1_, s0).astype(BF)
            base = pl.multiple_of(d * 256, 256)
            toep[pl.ds(base, HALF), 0:HALF] = a0
            toep[pl.ds(base + HALF, HALF), HALF:COLS] = a0
            toep[pl.ds(base + HALF, HALF), 0:HALF] = a1
            toep[pl.ds(base + 256, HALF), HALF:COLS] = a1
            prev = s1_
        return prev

    toep[0:HALF, HALF:COLS] = jnp.zeros((HALF, HALF), BF)
    lax.fori_loop(0, 32, build, jnp.zeros((HALF, HALF), F32))

    for c in cot_copies:
        c.wait()
    total = across(cot_all[0], w_ref[:, 0:256])
    for i in range(1, TP):
        total += across(cot_all[i], w_ref[:, 256 * i : 256 * i + 256])
    gy[...] = total
    send_l[...] = tiles_of((total * so[0]).astype(BF))
    scatter(send_l, recv_l, 2)

    first3 = iota((32, 8, HALF), 1) < 4

    def swap4(value):
        return pltpu.roll(value, 4, 1)

    def halves(ref):
        both = ref[...].astype(F32).reshape(32, 16, HALF)
        return both[:, 0:8], both[:, 8:16]

    def rows_of(one, two):
        return jnp.concatenate(
            [jnp.where(first3, one, swap4(two)), jnp.where(first3, swap4(one), two)], axis=2
        ).reshape(256, COLS)

    def backwards(value):
        return jnp.concatenate([value[31 - i : 32 - i] for i in range(32)], axis=0)

    def convolve(rows):
        for e in range(4):
            if e:
                stacked[:, 256 * e : 256 * e + 256] = jnp.concatenate(
                    [jnp.zeros((4 * e, COLS), F32), rows[: 256 - 4 * e]], axis=0
                ).astype(BF)
            else:
                stacked[:, 0:256] = rows.astype(BF)
        for n in range(16):
            term = plain(stacked[0 : 256 - 16 * n, :], toep[1024 * n : 1024 * n + 1024, :])
            if n:
                acc[16 * n : 256, :] += term
            else:
                acc[...] = term
        done = acc[...].reshape(32, 8, COLS)
        low = done[:, :, :HALF]
        high = done[:, :, HALF:]
        return jnp.where(first3, low, swap4(high)), jnp.where(first3, swap4(low), high)

    def give(ref, one, two):
        ref[...] = jnp.concatenate([one, two], axis=1).reshape(CTX, 8, HALF).astype(BF)

    wait_all(recv_g, 1, all_rcv)
    even, odd = halves(recv_g)
    rows_g = rows_of(even, odd)
    one, two = convolve(rows_g)
    give(ret_f, one, two)
    scatter(ret_f, back_f, 3)
    gct[...] = jnp.transpose(rows_g).astype(BF)

    wait_all(recv_l, 2, all_rcv)
    even, odd = halves(recv_l)
    one, two = convolve(rows_of(backwards(odd), backwards(even)))
    give(ret_b, backwards(two), backwards(one))
    scatter(ret_b, back_b, 4)

    slot_t = iota((COLS, 512), 1)
    chan_t = iota((COLS, 512), 0)
    home_t = (slot_t // 8) * 4 + lax.rem(slot_t, 8)
    take_a = one_hot((home_t == chan_t) & (lax.rem(slot_t, 8) < 4))
    take_b = one_hot((home_t == chan_t + 4) & (lax.rem(slot_t, 8) >= 4))
    same = flips[1]

    def channels(ref):
        got = ref[...].astype(F32).reshape(512, HALF).astype(BF)
        return jnp.concatenate([plain(take_a, got), plain(take_b, got)], axis=1).astype(BF)

    wait_all(back_f, 3, all_rcv)
    long_out = across(flips[0], channels(back_f))
    y_all = so[0] * long_out
    y_hi = y_all.astype(BF)
    y_lo = (y_all - y_hi.astype(F32)).astype(BF)
    y_t[0] = across(same, y_hi).astype(BF)
    y_t[1] = across(same, y_lo).astype(BF)
    off = pl.multiple_of(other * HALF, HALF)
    mine = pl.multiple_of(dp * HALF, HALF)
    pair_copies = []
    for i in range(TP):
        pair_out[i] = (
            plain(y_t[0, pl.ds(off, HALF), :], cot_all[i]) + plain(y_t[1, pl.ds(off, HALF), :], cot_all[i])
        ).astype(BF)
        c = copy(pair_out.at[i], pair_in.at[i], 8 + i, {"dp": other})
        c.start()
        pair_copies.append(c)
    for i in range(TP):
        part[:, 256 * i : 256 * i + 256] = plain(y_t[0, pl.ds(mine, HALF), :], cot_all[i]) + plain(
            y_t[1, pl.ds(mine, HALF), :], cot_all[i]
        )
    mix_copies = []
    for i in range(TP):
        mix_out[i] = (
            plain(y_hi, w_ref[:, 256 * i : 256 * i + 256]) + plain(y_lo, w_ref[:, 256 * i : 256 * i + 256])
        ).astype(BF)
    for k in range(1, TP):
        c = copy(mix_out.at[peer_tp(k)], mix_in.at[tp], 4 + k, {"tp": peer_tp(k)})
        c.start()
        mix_copies.append(c)

    for i in range(TP):
        pair_copies[i].wait()
        both = part[:, 256 * i : 256 * i + 256] + pair_in[i].astype(F32)
        for r in range(8):
            for h in range(2):
                sum_out[8 * r + 2 * i + h] = both[16 * r : 16 * r + 16, HALF * h : HALF * h + HALF].astype(BF)
    scatter(sum_out, sum_in, 6)

    wait_all(back_b, 4, all_rcv)
    grad_gated = across(same, channels(back_b))
    edge_out[6:8, :] = jnp.zeros((2, COLS), F32)
    sm0[0, 9:16, :] = jnp.zeros((7, COLS), F32)
    for i in range(3):
        gso = (gy[...] * long_out, grad_gated * so[2], grad_gated * so[1])[i]
        z1 = gso * masks[0]
        z2 = gso * masks[1]
        f0, f1, f2 = (taps_ref[i, s : s + 1, :] for s in range(TAPS))
        edge_out[2 * i : 2 * i + 1, :] = f2 * z2[0:1]
        edge_out[2 * i + 1 : 2 * i + 2, :] = f1 * z1[0:1] + f2 * z2[1:2]
        zbuf[0, 0:ROWS, :] = z1
        zbuf[1, 0:ROWS, :] = z2
        zbuf[:, ROWS : ROWS + 8, :] = jnp.zeros((2, 8, COLS), F32)
        sm0[0, 3 * i : 3 * i + 1, :] = jnp.sum(gso * xe[i, 8 : 8 + ROWS, :], axis=0, keepdims=True)
        sm0[0, 3 * i + 1 : 3 * i + 2, :] = jnp.sum(z1 * xe[i, 7 : 7 + ROWS, :], axis=0, keepdims=True)
        sm0[0, 3 * i + 2 : 3 * i + 3, :] = jnp.sum(z2 * xe[i, 6 : 6 + ROWS, :], axis=0, keepdims=True)
        xe[i, 0:ROWS, :] = f0 * gso + f1 * zbuf[0, 1 : 1 + ROWS, :] + f2 * zbuf[1, 2 : 2 + ROWS, :]
    edge_copy = copy(edge_out, edge_in, 15, {"ctx": peer_ctx(CTX - 1)})
    edge_copy.start()
    small_pair = copy(sm0.at[0], sm0.at[1], 16, {"dp": other})
    small_pair.start()

    straight = rows_of(even, odd)
    next_even = jnp.concatenate([even[1:], jnp.zeros((1, 8, HALF), F32)], axis=0)
    crossed = rows_of(odd, next_even)
    zero8 = jnp.zeros((8, COLS), F32)
    for n, value in enumerate(
        (straight, crossed, jnp.concatenate([straight[8:], zero8], axis=0), jnp.concatenate([crossed[8:], zero8], axis=0))
    ):
        gls[n, 0:256, :] = value.astype(BF)
        gls[n, 256:512, :] = jnp.zeros((256, COLS), BF)
    later = cols128 > rows128

    def roll_up(block):
        return pltpu.roll(block, 1, 1, stride=1, stride_axis=0)

    def lag_row(now, last):
        return jnp.sum(jnp.where(later, now, last), axis=0, keepdims=True).reshape(1, 1, HALF)

    def correlate(width):
        def body(m, carry):
            c11, last = carry
            for u in range(4):
                c = plain(gct[:, 0:width], gls[u, pl.ds(pl.multiple_of(16 * m, 16), width), :])
                r0 = roll_up(c11 + c[:HALF, :HALF])
                r1 = roll_up(c[:HALF, HALF:] + c[HALF:, :HALF])
                lag_out[pl.ds(8 * m + 2 * u, 1)] = lag_row(r0, last)
                lag_out[pl.ds(8 * m + 2 * u + 1, 1)] = lag_row(r1, r0)
                c11 = c[HALF:, HALF:]
                last = r1
            return c11, last

        return body

    nothing = jnp.zeros((HALF, HALF), F32)

    c11, last = lax.fori_loop(0, 8, correlate(256), (nothing, nothing))
    c11, last = lax.fori_loop(8, 16, correlate(128), (c11, last))
    r0 = roll_up(c11)
    lag_out[128:129] = lag_row(r0, last)
    lag_out[129:130] = lag_row(nothing, r0)

    def send_lags(k, carry):
        peer = peer_far(k)
        pltpu.make_async_remote_copy(
            lag_out.at[pl.ds(2 * peer + 2, 2)], lag_in.at[ctx], all_snd.at[5], all_rcv.at[5],
            device_id={"ctx": peer}, device_id_type=MESH,
        ).start()
        return carry

    lax.fori_loop(0, CTX - 1, send_lags, 0)
    lag_in[pl.ds(ctx, 1)] = lag_out[pl.ds(2 * ctx + 2, 2)].reshape(1, 2, 1, HALF)

    wait_all(sum_in, 6, all_rcv)
    total = sum_in[0].astype(F32)
    for n in range(1, CTX):
        total += sum_in[n].astype(F32)
    one_tile[...] = (total * scale).astype(BF)

    def share(k, carry):
        pltpu.make_async_remote_copy(
            one_tile, tiles.at[ctx], all_snd.at[7], grp.at[ctx // 16],
            device_id={"ctx": peer_far(k)}, device_id_type=MESH,
        ).start()
        return carry

    lax.fori_loop(0, CTX - 1, share, 0)
    pltpu.make_async_copy(one_tile, tiles.at[ctx], grp.at[ctx // 16]).start()

    small_pair.wait()
    sm1[0] = sm0[0] + sm0[1]
    small_first = []
    for k in range(1, 8):
        c = copy(sm1.at[0], sm1.at[k], 23 + k, dev1(k))
        c.start()
        small_first.append(c)
    edge_copy.wait()
    for i in range(3):
        xe[i, ROWS - 2 : ROWS, :] += edge_in[2 * i : 2 * i + 2, :]
        gin_ref[i] = xe[i, 0:ROWS, :].astype(BF)
    for c in mix_copies:
        c.wait()
    total = mix_out[pl.ds(tp, 1)].astype(F32)
    for k in range(1, TP):
        total += mix_in[pl.ds(peer_tp(k), 1)].astype(F32)
    mixed_ref[...] = total.reshape(ROWS, COLS).astype(BF)
    for c in small_first:
        c.wait()
    small = sm1[0]
    for k in range(1, 8):
        small += sm1[k]
    sm2[0] = small
    small_second = []
    for k in range(1, 8):
        c = copy(sm2.at[0], sm2.at[k], 38 + k, dev2(k))
        c.start()
        small_second.append(c)

    wait_all(lag_in, 5, all_rcv)
    for g in range(16):
        for h in range(2):
            value = lag_in[4 * g, h] + lag_in[4 * g + 1, h] + lag_in[4 * g + 2, h] + lag_in[4 * g + 3, h]
            lag_pair[0, g : g + 1, HALF * h : HALF * h + HALF] = value
    lag_copy = copy(lag_pair.at[0], lag_pair.at[1], 31, {"dp": other})
    lag_copy.start()

    last_copies = []
    for q in range(4):
        group = pl.ds(16 * q, 16)
        pltpu.make_async_copy(tiles.at[group], tiles.at[group], grp.at[q]).wait()
        c = copy(tiles.at[group], tiles_in.at[group], 17 + q, {"dp": other})
        c.start()
        last_copies.append(c)
    for q in range(CTX):
        gproj_ref[pl.ds(pl.multiple_of(mine + 16 * (q // 8), 16), 16), HALF * (q % 8) : HALF * (q % 8) + HALF] = tiles[q]
    lag_copy.wait()
    glong_ref[...] = (lag_pair[0] + lag_pair[1]) * scale
    for c in small_second:
        c.wait()
    small = sm2[0]
    for k in range(1, 8):
        small += sm2[k]
    small = small * scale
    for i in range(3):
        gtaps_ref[i] = small[3 * i : 3 * i + 3, :]
    for n, buf in enumerate((filt_in, send_g, send_l, ret_f, ret_b, lag_in, sum_in, tiles)):
        wait_all(buf, n, all_snd)
    for c in last_copies:
        c.wait()
    for q in range(CTX):
        gproj_ref[pl.ds(pl.multiple_of(off + 16 * (q // 8), 16), 16), HALF * (q % 8) : HALF * (q % 8) + HALF] = tiles_in[q]


def store(mixed, gin, gtaps, glong, gproj, mixed_o, gin_o, gtaps_o, glong_o, gproj_o, wide, sem):
    copies = []
    for n, (src, dst) in enumerate(((gin, gin_o), (mixed, mixed_o), (glong, glong_o), (gtaps, gtaps_o))):
        c = pltpu.make_async_copy(src, dst, sem.at[n])
        c.start()
        copies.append(c)
    for n in range(2):
        rows = pl.ds(HALF * n, HALF)
        wide[rows, :] = gproj[rows, :].astype(F32)
        c = pltpu.make_async_copy(wide.at[rows, :], gproj_o.at[rows, :], sem.at[4 + n])
        c.start()
        copies.append(c)
    for c in copies:
        c.wait()


def per_device(projected, segment_ids, short_filter, long_filter, out_proj, mixed_cotangent):
    scale = 1.0 / math.sqrt(2 * ROWS * CTX)
    V = pltpu.VMEM
    spec = pl.BlockSpec(memory_space=pltpu.VMEM)
    mixed, grad_in, grad_taps, grad_long, grad_proj = pl.pallas_call(
        functools.partial(layer, scale),
        out_shape=(
            jax.ShapeDtypeStruct((ROWS, COLS), BF),
            jax.ShapeDtypeStruct((3, ROWS, COLS), BF),
            jax.ShapeDtypeStruct((3, TAPS, COLS), F32),
            jax.ShapeDtypeStruct((16, COLS), F32),
            jax.ShapeDtypeStruct((256, 1024), BF),
        ),
        in_specs=[pl.BlockSpec(memory_space=pltpu.HBM)] * 6,
        out_specs=[spec] * 5,
        scratch_shapes=[
            V((3, ROWS, COLS), BF), V((1, ROWS), jnp.int32), V((3, TAPS, COLS), F32), V((16, COLS), F32), V((256, 1024), BF),
            pltpu.SemaphoreType.DMA((6,)), V((2, 512, COLS), BF), V((2, ROWS, ROWS), BF),
            V((TP, ROWS, COLS), BF), V((8, COLS), F32), V((8, COLS), F32),
            V((16, 1, COLS), F32), V((CTX, 1, COLS), F32),
            V((3, ROWS + 8, COLS), F32), V((3, ROWS, COLS), F32), V((2, ROWS, COLS), F32), V((ROWS, COLS), F32),
            V((CTX, 8, HALF), BF), V((CTX, 8, HALF), BF), V((CTX, 8, HALF), BF), V((CTX, 8, HALF), BF),
            V((64 * 256 + 256, 256), BF), V((256, 1024), BF), V((256, 256), F32),
            V((256, 256), BF), V((4, 512, 256), BF), V((130, 1, HALF), F32), V((CTX, 2, 1, HALF), F32),
            V((CTX, 8, HALF), BF), V((CTX, 8, HALF), BF), V((CTX, 8, HALF), BF), V((CTX, 8, HALF), BF),
            V((2, ROWS + 8, COLS), F32), V((2, COLS, ROWS), BF), V((HALF, 1024), F32),
            V((TP, ROWS, COLS), BF), V((TP, ROWS, COLS), BF),
            V((TP, HALF, COLS), BF), V((TP, HALF, COLS), BF),
            V((CTX, 16, HALF), BF), V((CTX, 16, HALF), BF), V((16, HALF), BF), V((CTX, 16, HALF), BF), V((CTX, 16, HALF), BF),
            V((2, 16, COLS), F32), V((8, 16, COLS), F32), V((8, 16, COLS), F32),
            V((8, COLS), F32), V((8, COLS), F32), V((2, 16, COLS), F32),
            pltpu.SemaphoreType.DMA((46,)), pltpu.SemaphoreType.DMA((46,)),
            pltpu.SemaphoreType.DMA((8,)), pltpu.SemaphoreType.DMA((8,)), pltpu.SemaphoreType.DMA((4,)),
        ],
        compiler_params=pltpu.CompilerParams(vmem_limit_bytes=48 << 20, collective_id=0, has_side_effects=True),
        name="layer",
    )(*(pltpu.with_memory_space_constraint(v, pltpu.HBM) for v in (projected[:, 0], segment_ids, short_filter, long_filter, out_proj, mixed_cotangent[0])))
    mixed, grad_in, grad_taps, grad_long, grad_proj = pl.pallas_call(
        store,
        out_shape=(
            jax.ShapeDtypeStruct((ROWS, COLS), BF),
            jax.ShapeDtypeStruct((3, ROWS, COLS), BF),
            jax.ShapeDtypeStruct((3, TAPS, COLS), F32),
            jax.ShapeDtypeStruct((16, COLS), F32),
            jax.ShapeDtypeStruct((256, 1024), F32),
        ),
        in_specs=[spec] * 5,
        out_specs=[pl.BlockSpec(memory_space=pltpu.HBM)] * 5,
        scratch_shapes=[V((256, 1024), F32), pltpu.SemaphoreType.DMA((6,))],
        compiler_params=pltpu.CompilerParams(vmem_limit_bytes=8 << 20),
        name="store",
    )(mixed, grad_in, grad_taps, grad_long, grad_proj)
    return (mixed[None], grad_in[:, None], grad_taps, grad_long, grad_proj)


def solution(mesh):
    in_specs = (
        P(None, "dp", "ctx", "tp"),
        P("dp", "ctx"),
        P(None, None, "tp"),
        P("tp", "ctx"),
        P("tp", None),
        P("dp", "ctx", "tp"),
    )
    out_specs = (
        P("dp", "ctx", "tp"),
        P(None, "dp", "ctx", "tp"),
        P(None, None, "tp"),
        P("tp", "ctx"),
        P("tp", None),
    )
    return jax.shard_map(
        per_device, mesh=mesh, in_specs=in_specs, out_specs=out_specs, check_vma=False
    )
```

```python
import functools
import math

import jax
import jax.numpy as jnp
from jax import lax
from jax.experimental import pallas as pl
from jax.experimental.pallas import tpu as pltpu
from jax.sharding import PartitionSpec as P

F32 = jnp.float32
BF = jnp.bfloat16
MESH = pl.DeviceIdType.MESH
CTX = 64
TP = 4
TAPS = 3
ROWS = 256
COLS = 256
HALF = 128


def iota(shape, axis):
    return lax.broadcasted_iota(jnp.int32, shape, axis)


def one_hot(condition):
    return jnp.where(condition, 1.0, 0.0).astype(BF)


def across(a, b):
    return lax.dot_general(a, b, (((1,), (1,)), ((), ())), preferred_element_type=F32)


def plain(a, b):
    return jnp.dot(a, b, preferred_element_type=F32)


def layer(
    scale,
    x_hbm, seg_hbm, taps_hbm, filt_hbm, w_hbm, cot_hbm,
    mixed_ref, gin_ref, gtaps_ref, glong_ref, gproj_ref,
    x_ref, seg_ref, taps_ref, filt_ref, w_ref, load_sem, picks, flips,
    cot_all, halo_out, halo_in, filt_out, filt_in, xe, so, masks, gy,
    send_g, recv_g, send_l, recv_l, toep, stacked, acc, gct, gls, kept, lag_out, lag_in,
    ret_f, back_f, ret_b, back_b, zbuf, y_t, part, mix_out, mix_in,
    pair_out, pair_in, sum_out, sum_in, one_tile, tiles, tiles_in,
    sm0, sm1, sm2, edge_out, edge_in, lag_pair,
    snd, rcv, all_snd, all_rcv, grp,
):
    ctx = lax.axis_index("ctx")
    tp = lax.axis_index("tp")
    dp = lax.axis_index("dp")
    y = lax.rem(ctx, 8)
    z = ctx // 8
    my1 = y * (1 - dp) + z * dp
    my2 = z * (1 - dp) + y * dp
    step1 = 1 + 7 * dp
    step2 = 8 - 7 * dp
    base1 = ctx - my1 * step1
    base2 = ctx - my2 * step2
    other = 1 - dp

    def peer1(k):
        return lax.rem(my1 + k, 8)

    def dev1(k):
        return {"ctx": base1 + peer1(k) * step1}

    def peer2(k):
        return lax.rem(my2 + k, 8)

    def dev2(k):
        return {"ctx": base2 + peer2(k) * step2}

    def peer_tp(k):
        return lax.rem(tp + k, TP)

    def peer_ctx(k):
        return lax.rem(ctx + k, CTX)

    def peer_nth(k):
        return lax.rem(ctx + k + 1, CTX)

    def copy(src, dst, n, dev):
        return pltpu.make_async_remote_copy(
            src, dst, snd.at[n], rcv.at[n], device_id=dev, device_id_type=MESH
        )

    barrier = pltpu.get_barrier_semaphore()

    def greet(k, carry):
        pl.semaphore_signal(barrier, 1, device_id={"ctx": peer_nth(k)}, device_id_type=MESH)
        return carry

    for k in range(1, TP):
        pl.semaphore_signal(barrier, 1, device_id={"tp": peer_tp(k)}, device_id_type=MESH)
    pl.semaphore_signal(barrier, 1, device_id={"dp": other}, device_id_type=MESH)
    lax.fori_loop(0, CTX - 1, greet, 0)
    loads = []
    for n, (src, dst) in enumerate((
        (filt_hbm, filt_ref), (seg_hbm, seg_ref), (x_hbm, x_ref),
        (cot_hbm, cot_all.at[tp]), (taps_hbm, taps_ref), (w_hbm, w_ref),
    )):
        load = pltpu.make_async_copy(src, dst, load_sem.at[n])
        load.start()
        loads.append(load)

    for load in loads[:3]:
        load.wait()
    rows128 = iota((HALF, HALF), 0)
    cols128 = iota((HALF, HALF), 1)
    flip128 = one_hot(rows128 + cols128 == HALF - 1)
    filt = filt_ref[...].astype(BF)
    filt_out[...] = jnp.concatenate(
        [plain(filt[:, :HALF], flip128), plain(filt[:, HALF:], flip128)], axis=1
    ).reshape(16, 1, COLS)
    seg_row = seg_ref[...].astype(F32)
    seg_col = jnp.transpose(jnp.broadcast_to(seg_row, (HALF, ROWS)))
    halo_out[0:6, :] = jnp.concatenate([x_ref[i, ROWS - 2 : ROWS, :].astype(F32) for i in range(3)], axis=0)
    halo_out[6:8, :] = jnp.concatenate([seg_col[ROWS - 2 : ROWS, :]] * 2, axis=1)
    slot = iota((512, COLS), 0)
    chan = iota((512, COLS), 1)
    home = (slot // 8) * 4 + lax.rem(slot, 8)
    picks[0] = one_hot((home == chan) & (lax.rem(slot, 8) < 4))
    picks[1] = one_hot((home == chan + 4) & (lax.rem(slot, 8) >= 4))
    flips[0] = one_hot(iota((ROWS, ROWS), 0) + iota((ROWS, ROWS), 1) == ROWS - 1)
    flips[1] = one_hot(iota((ROWS, ROWS), 0) == iota((ROWS, ROWS), 1))
    for i in range(3):
        xe[i, 8 : 8 + ROWS, :] = x_ref[i].astype(F32)
    loads[3].wait()
    pl.semaphore_wait(barrier, CTX - 1 + TP - 1 + 1)

    halo = copy(halo_out, halo_in, 0, {"ctx": peer_ctx(1)})
    halo.start()
    cot_copies = []
    for k in range(1, TP):
        c = copy(cot_all.at[tp], cot_all.at[tp], k, {"tp": peer_tp(k)})
        c.start()
        cot_copies.append(c)

    def send_filter(k, carry):
        peer = peer_nth(k)
        pltpu.make_async_remote_copy(
            filt_out.at[peer // 4], filt_in.at[ctx], all_snd.at[0], all_rcv.at[0],
            device_id={"ctx": peer}, device_id_type=MESH,
        ).start()
        return carry

    lax.fori_loop(0, CTX - 1, send_filter, 0)
    filt_in[pl.ds(ctx, 1)] = filt_out[pl.ds(ctx // 4, 1)]

    def wait_all(buf, n, which):
        pltpu.make_async_copy(buf.at[pl.ds(0, CTX - 1)], buf.at[pl.ds(0, CTX - 1)], which.at[n]).wait()

    halo.wait()
    loads[4].wait()
    loads[5].wait()

    for i in range(3):
        xe[i, 6:8, :] = halo_in[2 * i : 2 * i + 2, :]
    prev_seg = jnp.where(ctx == 0, -1.0, halo_in[6:8, 0:HALF])
    before1 = jnp.concatenate([prev_seg[1:2], seg_col[: ROWS - 1]], axis=0)
    before2 = jnp.concatenate([prev_seg, seg_col[: ROWS - 2]], axis=0)
    for n, before in enumerate((before1, before2)):
        mask = jnp.where(before == seg_col, 1.0, 0.0)
        masks[n] = jnp.concatenate([mask, mask], axis=1)

    def featurize(i):
        so[i] = (
            taps_ref[i, 0:1, :] * xe[i, 8 : 8 + ROWS, :]
            + taps_ref[i, 1:2, :] * masks[0] * xe[i, 7 : 7 + ROWS, :]
            + taps_ref[i, 2:3, :] * masks[1] * xe[i, 6 : 6 + ROWS, :]
        )

    featurize(1)
    featurize(2)

    def scatter(src, dst, n):
        def one(k, carry):
            peer = peer_nth(k)
            pltpu.make_async_remote_copy(
                src.at[peer], dst.at[ctx], all_snd.at[n], all_rcv.at[n],
                device_id={"ctx": peer}, device_id_type=MESH,
            ).start()
            return carry

        lax.fori_loop(0, CTX - 1, one, 0)
        dst[pl.ds(ctx, 1)] = src[pl.ds(ctx, 1)]

    def tiles_of(value):
        return (across(picks[0], value[:HALF]) + across(picks[1], value[HALF:])).reshape(CTX, 8, HALF).astype(BF)

    send_g[...] = tiles_of(plain(flips[0], (so[1] * so[2]).astype(BF)).astype(BF))
    scatter(send_g, recv_g, 1)
    featurize(0)

    wait_all(filt_in, 0, all_rcv)
    keep = rows128 >= cols128

    def spread(line):
        return pltpu.roll(jnp.broadcast_to(line, (HALF, HALF)), 1, 1, stride=1, stride_axis=0)

    def build(n, prev):
        for u in range(2):
            d = 2 * n + u
            line = filt_in[d]
            s0 = spread(line[:, :HALF])
            a0 = jnp.where(keep, s0, prev).astype(BF)
            s1_ = spread(line[:, HALF:])
            a1 = jnp.where(keep, s1_, s0).astype(BF)
            base = pl.multiple_of(d * 256, 256)
            toep[pl.ds(base, HALF), 0:HALF] = a0
            toep[pl.ds(base + HALF, HALF), HALF:COLS] = a0
            toep[pl.ds(base + HALF, HALF), 0:HALF] = a1
            toep[pl.ds(base + 256, HALF), HALF:COLS] = a1
            prev = s1_
        return prev

    toep[0:HALF, HALF:COLS] = jnp.zeros((HALF, HALF), BF)
    lax.fori_loop(0, 32, build, jnp.zeros((HALF, HALF), F32))

    for c in cot_copies:
        c.wait()
    total = across(cot_all[0], w_ref[:, 0:256])
    for i in range(1, TP):
        total += across(cot_all[i], w_ref[:, 256 * i : 256 * i + 256])
    gy[...] = total
    send_l[...] = tiles_of((total * so[0]).astype(BF))
    scatter(send_l, recv_l, 2)

    first3 = iota((32, 8, HALF), 1) < 4

    def swap4(value):
        return pltpu.roll(value, 4, 1)

    def halves(ref):
        both = ref[...].astype(F32).reshape(32, 16, HALF)
        return both[:, 0:8], both[:, 8:16]

    def rows_of(one, two):
        return jnp.concatenate(
            [jnp.where(first3, one, swap4(two)), jnp.where(first3, swap4(one), two)], axis=2
        ).reshape(256, COLS)

    def backwards(value):
        return jnp.concatenate([value[31 - i : 32 - i] for i in range(32)], axis=0)

    def convolve(rows):
        for e in range(4):
            if e:
                stacked[:, 256 * e : 256 * e + 256] = jnp.concatenate(
                    [jnp.zeros((4 * e, COLS), F32), rows[: 256 - 4 * e]], axis=0
                ).astype(BF)
            else:
                stacked[:, 0:256] = rows.astype(BF)
        for n in range(16):
            term = plain(stacked[0 : 256 - 16 * n, :], toep[1024 * n : 1024 * n + 1024, :])
            if n:
                acc[16 * n : 256, :] += term
            else:
                acc[...] = term
        done = acc[...].reshape(32, 8, COLS)
        low = done[:, :, :HALF]
        high = done[:, :, HALF:]
        return jnp.where(first3, low, swap4(high)), jnp.where(first3, swap4(low), high)

    def give(ref, one, two):
        ref[...] = jnp.concatenate([one, two], axis=1).reshape(CTX, 8, HALF).astype(BF)

    wait_all(recv_g, 1, all_rcv)
    even, odd = halves(recv_g)
    rows_g = rows_of(even, odd)
    one, two = convolve(rows_g)
    give(ret_f, one, two)
    scatter(ret_f, back_f, 3)
    gct[...] = jnp.transpose(rows_g).astype(BF)

    wait_all(recv_l, 2, all_rcv)
    even, odd = halves(recv_l)
    one, two = convolve(rows_of(backwards(odd), backwards(even)))
    give(ret_b, backwards(two), backwards(one))
    scatter(ret_b, back_b, 4)

    slot_t = iota((COLS, 512), 1)
    chan_t = iota((COLS, 512), 0)
    home_t = (slot_t // 8) * 4 + lax.rem(slot_t, 8)
    take_a = one_hot((home_t == chan_t) & (lax.rem(slot_t, 8) < 4))
    take_b = one_hot((home_t == chan_t + 4) & (lax.rem(slot_t, 8) >= 4))
    same = flips[1]

    def channels(ref):
        got = ref[...].astype(F32).reshape(512, HALF).astype(BF)
        return jnp.concatenate([plain(take_a, got), plain(take_b, got)], axis=1).astype(BF)

    wait_all(back_f, 3, all_rcv)
    long_out = across(flips[0], channels(back_f))
    y_all = so[0] * long_out
    y_hi = y_all.astype(BF)
    y_lo = (y_all - y_hi.astype(F32)).astype(BF)
    y_t[0] = across(same, y_hi).astype(BF)
    y_t[1] = across(same, y_lo).astype(BF)
    off = pl.multiple_of(other * HALF, HALF)
    mine = pl.multiple_of(dp * HALF, HALF)
    pair_copies = []
    for i in range(TP):
        pair_out[i] = (
            plain(y_t[0, pl.ds(off, HALF), :], cot_all[i]) + plain(y_t[1, pl.ds(off, HALF), :], cot_all[i])
        ).astype(BF)
        c = copy(pair_out.at[i], pair_in.at[i], 8 + i, {"dp": other})
        c.start()
        pair_copies.append(c)
    for i in range(TP):
        part[:, 256 * i : 256 * i + 256] = plain(y_t[0, pl.ds(mine, HALF), :], cot_all[i]) + plain(
            y_t[1, pl.ds(mine, HALF), :], cot_all[i]
        )
    mix_copies = []
    for i in range(TP):
        mix_out[i] = (
            plain(y_hi, w_ref[:, 256 * i : 256 * i + 256]) + plain(y_lo, w_ref[:, 256 * i : 256 * i + 256])
        ).astype(BF)
    for k in range(1, TP):
        c = copy(mix_out.at[peer_tp(k)], mix_in.at[tp], 4 + k, {"tp": peer_tp(k)})
        c.start()
        mix_copies.append(c)

    for i in range(TP):
        pair_copies[i].wait()
        both = part[:, 256 * i : 256 * i + 256] + pair_in[i].astype(F32)
        for r in range(8):
            for h in range(2):
                sum_out[8 * r + 2 * i + h] = both[16 * r : 16 * r + 16, HALF * h : HALF * h + HALF].astype(BF)
    scatter(sum_out, sum_in, 6)

    wait_all(back_b, 4, all_rcv)
    grad_gated = across(same, channels(back_b))
    edge_out[6:8, :] = jnp.zeros((2, COLS), F32)
    sm0[0, 9:16, :] = jnp.zeros((7, COLS), F32)
    for i in range(3):
        gso = (gy[...] * long_out, grad_gated * so[2], grad_gated * so[1])[i]
        z1 = gso * masks[0]
        z2 = gso * masks[1]
        f0, f1, f2 = (taps_ref[i, s : s + 1, :] for s in range(TAPS))
        edge_out[2 * i : 2 * i + 1, :] = f2 * z2[0:1]
        edge_out[2 * i + 1 : 2 * i + 2, :] = f1 * z1[0:1] + f2 * z2[1:2]
        zbuf[0, 0:ROWS, :] = z1
        zbuf[1, 0:ROWS, :] = z2
        zbuf[:, ROWS : ROWS + 8, :] = jnp.zeros((2, 8, COLS), F32)
        sm0[0, 3 * i : 3 * i + 1, :] = jnp.sum(gso * xe[i, 8 : 8 + ROWS, :], axis=0, keepdims=True)
        sm0[0, 3 * i + 1 : 3 * i + 2, :] = jnp.sum(z1 * xe[i, 7 : 7 + ROWS, :], axis=0, keepdims=True)
        sm0[0, 3 * i + 2 : 3 * i + 3, :] = jnp.sum(z2 * xe[i, 6 : 6 + ROWS, :], axis=0, keepdims=True)
        xe[i, 0:ROWS, :] = f0 * gso + f1 * zbuf[0, 1 : 1 + ROWS, :] + f2 * zbuf[1, 2 : 2 + ROWS, :]
    edge_copy = copy(edge_out, edge_in, 15, {"ctx": peer_ctx(CTX - 1)})
    edge_copy.start()
    small_pair = copy(sm0.at[0], sm0.at[1], 16, {"dp": other})
    small_pair.start()

    straight = rows_of(even, odd)
    next_even = jnp.concatenate([even[1:], jnp.zeros((1, 8, HALF), F32)], axis=0)
    crossed = rows_of(odd, next_even)
    zero8 = jnp.zeros((8, COLS), F32)
    for n, value in enumerate(
        (straight, crossed, jnp.concatenate([straight[8:], zero8], axis=0), jnp.concatenate([crossed[8:], zero8], axis=0))
    ):
        gls[n, 0:256, :] = value.astype(BF)
        gls[n, 256:512, :] = jnp.zeros((256, COLS), BF)
    later = cols128 > rows128

    def roll_up(block):
        return pltpu.roll(block, 1, 1, stride=1, stride_axis=0)

    def lag_row(now, last):
        return jnp.sum(jnp.where(later, now, last), axis=0, keepdims=True).reshape(1, 1, HALF)

    def correlate(width):
        def body(m, carry):
            c11, last = carry
            for u in range(4):
                c = plain(gct[:, 0:width], gls[u, pl.ds(pl.multiple_of(16 * m, 16), width), :])
                r0 = roll_up(c11 + c[:HALF, :HALF])
                r1 = roll_up(c[:HALF, HALF:] + c[HALF:, :HALF])
                lag_out[pl.ds(8 * m + 2 * u, 1)] = lag_row(r0, last)
                lag_out[pl.ds(8 * m + 2 * u + 1, 1)] = lag_row(r1, r0)
                c11 = c[HALF:, HALF:]
                last = r1
            return c11, last

        return body

    nothing = jnp.zeros((HALF, HALF), F32)

    c11, last = lax.fori_loop(0, 8, correlate(256), (nothing, nothing))
    kept[0] = c11
    kept[1] = last

    wait_all(sum_in, 6, all_rcv)
    total = sum_in[0].astype(F32)
    for n in range(1, CTX):
        total += sum_in[n].astype(F32)
    one_tile[...] = (total * scale).astype(BF)

    def share(k, carry):
        pltpu.make_async_remote_copy(
            one_tile, tiles.at[ctx], all_snd.at[7], grp.at[ctx // 16],
            device_id={"ctx": peer_nth(k)}, device_id_type=MESH,
        ).start()
        return carry

    lax.fori_loop(0, CTX - 1, share, 0)
    pltpu.make_async_copy(one_tile, tiles.at[ctx], grp.at[ctx // 16]).start()

    small_pair.wait()
    sm1[0] = sm0[0] + sm0[1]
    small_first = []
    for k in range(1, 8):
        c = copy(sm1.at[0], sm1.at[k], 23 + k, dev1(k))
        c.start()
        small_first.append(c)
    c11, last = lax.fori_loop(8, 16, correlate(128), (kept[0], kept[1]))
    r0 = roll_up(c11)
    lag_out[128:129] = lag_row(r0, last)
    lag_out[129:130] = lag_row(nothing, r0)

    def send_lags(k, carry):
        peer = peer_nth(k)
        pltpu.make_async_remote_copy(
            lag_out.at[pl.ds(2 * peer + 2, 2)], lag_in.at[ctx], all_snd.at[5], all_rcv.at[5],
            device_id={"ctx": peer}, device_id_type=MESH,
        ).start()
        return carry

    lax.fori_loop(0, CTX - 1, send_lags, 0)
    lag_in[pl.ds(ctx, 1)] = lag_out[pl.ds(2 * ctx + 2, 2)].reshape(1, 2, 1, HALF)
    edge_copy.wait()
    for i in range(3):
        xe[i, ROWS - 2 : ROWS, :] += edge_in[2 * i : 2 * i + 2, :]
        gin_ref[i] = xe[i, 0:ROWS, :].astype(BF)
    for c in mix_copies:
        c.wait()
    total = mix_out[pl.ds(tp, 1)].astype(F32)
    for k in range(1, TP):
        total += mix_in[pl.ds(peer_tp(k), 1)].astype(F32)
    mixed_ref[...] = total.reshape(ROWS, COLS).astype(BF)
    for c in small_first:
        c.wait()
    small = sm1[0]
    for k in range(1, 8):
        small += sm1[k]
    sm2[0] = small
    small_second = []
    for k in range(1, 8):
        c = copy(sm2.at[0], sm2.at[k], 38 + k, dev2(k))
        c.start()
        small_second.append(c)

    wait_all(lag_in, 5, all_rcv)
    for g in range(16):
        for h in range(2):
            value = lag_in[4 * g, h] + lag_in[4 * g + 1, h] + lag_in[4 * g + 2, h] + lag_in[4 * g + 3, h]
            lag_pair[0, g : g + 1, HALF * h : HALF * h + HALF] = value
    lag_copy = copy(lag_pair.at[0], lag_pair.at[1], 31, {"dp": other})
    lag_copy.start()

    last_copies = []
    for q in range(4):
        group = pl.ds(16 * q, 16)
        pltpu.make_async_copy(tiles.at[group], tiles.at[group], grp.at[q]).wait()
        c = copy(tiles.at[group], tiles_in.at[group], 17 + q, {"dp": other})
        c.start()
        last_copies.append(c)
    for q in range(CTX):
        gproj_ref[pl.ds(pl.multiple_of(mine + 16 * (q // 8), 16), 16), HALF * (q % 8) : HALF * (q % 8) + HALF] = tiles[q]
    lag_copy.wait()
    glong_ref[...] = (lag_pair[0] + lag_pair[1]) * scale
    for c in small_second:
        c.wait()
    small = sm2[0]
    for k in range(1, 8):
        small += sm2[k]
    small = small * scale
    for i in range(3):
        gtaps_ref[i] = small[3 * i : 3 * i + 3, :]
    for n, buf in enumerate((filt_in, send_g, send_l, ret_f, ret_b, lag_in, sum_in, tiles)):
        wait_all(buf, n, all_snd)
    for c in last_copies:
        c.wait()
    for q in range(CTX):
        gproj_ref[pl.ds(pl.multiple_of(off + 16 * (q // 8), 16), 16), HALF * (q % 8) : HALF * (q % 8) + HALF] = tiles_in[q]


def store(mixed, gin, gtaps, glong, gproj, mixed_o, gin_o, gtaps_o, glong_o, gproj_o, wide, sem):
    copies = []
    for n, (src, dst) in enumerate(((gin, gin_o), (mixed, mixed_o), (glong, glong_o), (gtaps, gtaps_o))):
        c = pltpu.make_async_copy(src, dst, sem.at[n])
        c.start()
        copies.append(c)
    for n in range(2):
        rows = pl.ds(HALF * n, HALF)
        wide[rows, :] = gproj[rows, :].astype(F32)
        c = pltpu.make_async_copy(wide.at[rows, :], gproj_o.at[rows, :], sem.at[4 + n])
        c.start()
        copies.append(c)
    for c in copies:
        c.wait()


def per_device(projected, segment_ids, short_filter, long_filter, out_proj, mixed_cotangent):
    scale = 1.0 / math.sqrt(2 * ROWS * CTX)
    V = pltpu.VMEM
    spec = pl.BlockSpec(memory_space=pltpu.VMEM)
    mixed, grad_in, grad_taps, grad_long, grad_proj = pl.pallas_call(
        functools.partial(layer, scale),
        out_shape=(
            jax.ShapeDtypeStruct((ROWS, COLS), BF),
            jax.ShapeDtypeStruct((3, ROWS, COLS), BF),
            jax.ShapeDtypeStruct((3, TAPS, COLS), F32),
            jax.ShapeDtypeStruct((16, COLS), F32),
            jax.ShapeDtypeStruct((256, 1024), BF),
        ),
        in_specs=[pl.BlockSpec(memory_space=pltpu.HBM)] * 6,
        out_specs=[spec] * 5,
        scratch_shapes=[
            V((3, ROWS, COLS), BF), V((1, ROWS), jnp.int32), V((3, TAPS, COLS), F32), V((16, COLS), F32), V((256, 1024), BF),
            pltpu.SemaphoreType.DMA((6,)), V((2, 512, COLS), BF), V((2, ROWS, ROWS), BF),
            V((TP, ROWS, COLS), BF), V((8, COLS), F32), V((8, COLS), F32),
            V((16, 1, COLS), F32), V((CTX, 1, COLS), F32),
            V((3, ROWS + 8, COLS), F32), V((3, ROWS, COLS), F32), V((2, ROWS, COLS), F32), V((ROWS, COLS), F32),
            V((CTX, 8, HALF), BF), V((CTX, 8, HALF), BF), V((CTX, 8, HALF), BF), V((CTX, 8, HALF), BF),
            V((64 * 256 + 256, 256), BF), V((256, 1024), BF), V((256, 256), F32),
            V((256, 256), BF), V((4, 512, 256), BF), V((2, HALF, HALF), F32), V((130, 1, HALF), F32), V((CTX, 2, 1, HALF), F32),
            V((CTX, 8, HALF), BF), V((CTX, 8, HALF), BF), V((CTX, 8, HALF), BF), V((CTX, 8, HALF), BF),
            V((2, ROWS + 8, COLS), F32), V((2, COLS, ROWS), BF), V((HALF, 1024), F32),
            V((TP, ROWS, COLS), BF), V((TP, ROWS, COLS), BF),
            V((TP, HALF, COLS), BF), V((TP, HALF, COLS), BF),
            V((CTX, 16, HALF), BF), V((CTX, 16, HALF), BF), V((16, HALF), BF), V((CTX, 16, HALF), BF), V((CTX, 16, HALF), BF),
            V((2, 16, COLS), F32), V((8, 16, COLS), F32), V((8, 16, COLS), F32),
            V((8, COLS), F32), V((8, COLS), F32), V((2, 16, COLS), F32),
            pltpu.SemaphoreType.DMA((46,)), pltpu.SemaphoreType.DMA((46,)),
            pltpu.SemaphoreType.DMA((8,)), pltpu.SemaphoreType.DMA((8,)), pltpu.SemaphoreType.DMA((4,)),
        ],
        compiler_params=pltpu.CompilerParams(vmem_limit_bytes=48 << 20, collective_id=0, has_side_effects=True),
        name="layer",
    )(*(pltpu.with_memory_space_constraint(v, pltpu.HBM) for v in (projected[:, 0], segment_ids, short_filter, long_filter, out_proj, mixed_cotangent[0])))
    mixed, grad_in, grad_taps, grad_long, grad_proj = pl.pallas_call(
        store,
        out_shape=(
            jax.ShapeDtypeStruct((ROWS, COLS), BF),
            jax.ShapeDtypeStruct((3, ROWS, COLS), BF),
            jax.ShapeDtypeStruct((3, TAPS, COLS), F32),
            jax.ShapeDtypeStruct((16, COLS), F32),
            jax.ShapeDtypeStruct((256, 1024), F32),
        ),
        in_specs=[spec] * 5,
        out_specs=[pl.BlockSpec(memory_space=pltpu.HBM)] * 5,
        scratch_shapes=[V((256, 1024), F32), pltpu.SemaphoreType.DMA((6,))],
        compiler_params=pltpu.CompilerParams(vmem_limit_bytes=8 << 20),
        name="store",
    )(mixed, grad_in, grad_taps, grad_long, grad_proj)
    return (mixed[None], grad_in[:, None], grad_taps, grad_long, grad_proj)


def solution(mesh):
    in_specs = (
        P(None, "dp", "ctx", "tp"),
        P("dp", "ctx"),
        P(None, None, "tp"),
        P("tp", "ctx"),
        P("tp", None),
        P("dp", "ctx", "tp"),
    )
    out_specs = (
        P("dp", "ctx", "tp"),
        P(None, "dp", "ctx", "tp"),
        P(None, None, "tp"),
        P("tp", "ctx"),
        P("tp", None),
    )
    return jax.shard_map(
        per_device, mesh=mesh, in_specs=in_specs, out_specs=out_specs, check_vma=False
    )
```

```python
import functools
import math

import jax
import jax.numpy as jnp
from jax import lax
from jax.experimental import pallas as pl
from jax.experimental.pallas import tpu as pltpu
from jax.sharding import PartitionSpec as P

F32 = jnp.float32
BF = jnp.bfloat16
MESH = pl.DeviceIdType.MESH
CTX = 64
TP = 4
TAPS = 3
ROWS = 256
COLS = 256
HALF = 128


def iota(shape, axis):
    return lax.broadcasted_iota(jnp.int32, shape, axis)


def one_hot(condition):
    return jnp.where(condition, 1.0, 0.0).astype(BF)


def across(a, b):
    return lax.dot_general(a, b, (((1,), (1,)), ((), ())), preferred_element_type=F32)


def plain(a, b):
    return jnp.dot(a, b, preferred_element_type=F32)


def layer(
    scale,
    x_hbm, seg_hbm, taps_hbm, filt_hbm, w_hbm, cot_hbm,
    mixed_ref, gin_ref, gtaps_ref, glong_ref, gproj_ref,
    x_ref, seg_ref, taps_ref, filt_ref, w_ref, load_sem, picks, flips,
    cot_all, halo_out, halo_in, filt_out, filt_in, xe, so, masks, gy,
    send_g, recv_g, send_l, recv_l, toep, stacked, acc, gct, gls, lag_out, lag_in,
    ret_f, back_f, ret_b, back_b, zbuf, y_t, part, mix_out, mix_in,
    pair_out, pair_in, sum_out, sum_in, one_tile, tiles, tiles_in,
    sm0, sm1, sm2, edge_out, edge_in, lag_pair,
    snd, rcv, all_snd, all_rcv, grp,
):
    ctx = lax.axis_index("ctx")
    tp = lax.axis_index("tp")
    dp = lax.axis_index("dp")
    y = lax.rem(ctx, 8)
    z = ctx // 8
    my1 = y * (1 - dp) + z * dp
    my2 = z * (1 - dp) + y * dp
    step1 = 1 + 7 * dp
    step2 = 8 - 7 * dp
    base1 = ctx - my1 * step1
    base2 = ctx - my2 * step2
    other = 1 - dp

    def peer1(k):
        return lax.rem(my1 + k, 8)

    def dev1(k):
        return {"ctx": base1 + peer1(k) * step1}

    def peer2(k):
        return lax.rem(my2 + k, 8)

    def dev2(k):
        return {"ctx": base2 + peer2(k) * step2}

    def peer_tp(k):
        return lax.rem(tp + k, TP)

    def peer_ctx(k):
        return lax.rem(ctx + k, CTX)

    def peer_nth(k):
        return lax.rem(ctx + k + 1, CTX)

    def copy(src, dst, n, dev):
        return pltpu.make_async_remote_copy(
            src, dst, snd.at[n], rcv.at[n], device_id=dev, device_id_type=MESH
        )

    barrier = pltpu.get_barrier_semaphore()

    def greet(k, carry):
        pl.semaphore_signal(barrier, 1, device_id={"ctx": peer_nth(k)}, device_id_type=MESH)
        return carry

    for k in range(1, TP):
        pl.semaphore_signal(barrier, 1, device_id={"tp": peer_tp(k)}, device_id_type=MESH)
    pl.semaphore_signal(barrier, 1, device_id={"dp": other}, device_id_type=MESH)
    lax.fori_loop(0, CTX - 1, greet, 0)
    loads = []
    for n, (src, dst) in enumerate((
        (filt_hbm, filt_ref), (seg_hbm, seg_ref), (x_hbm, x_ref),
        (cot_hbm, cot_all.at[tp]), (taps_hbm, taps_ref), (w_hbm, w_ref),
    )):
        load = pltpu.make_async_copy(src, dst, load_sem.at[n])
        load.start()
        loads.append(load)

    for load in loads[:3]:
        load.wait()
    rows128 = iota((HALF, HALF), 0)
    cols128 = iota((HALF, HALF), 1)
    flip128 = one_hot(rows128 + cols128 == HALF - 1)
    filt = filt_ref[...].astype(BF)
    filt_out[...] = jnp.concatenate(
        [plain(filt[:, :HALF], flip128), plain(filt[:, HALF:], flip128)], axis=1
    ).reshape(16, 1, COLS)
    seg_row = seg_ref[...].astype(F32)
    seg_col = jnp.transpose(jnp.broadcast_to(seg_row, (HALF, ROWS)))
    halo_out[0:6, :] = jnp.concatenate([x_ref[i, ROWS - 2 : ROWS, :].astype(F32) for i in range(3)], axis=0)
    halo_out[6:8, :] = jnp.concatenate([seg_col[ROWS - 2 : ROWS, :]] * 2, axis=1)
    slot = iota((512, COLS), 0)
    chan = iota((512, COLS), 1)
    home = (slot // 8) * 4 + lax.rem(slot, 8)
    picks[0] = one_hot((home == chan) & (lax.rem(slot, 8) < 4))
    picks[1] = one_hot((home == chan + 4) & (lax.rem(slot, 8) >= 4))
    flips[0] = one_hot(iota((ROWS, ROWS), 0) + iota((ROWS, ROWS), 1) == ROWS - 1)
    flips[1] = one_hot(iota((ROWS, ROWS), 0) == iota((ROWS, ROWS), 1))
    for i in range(3):
        xe[i, 8 : 8 + ROWS, :] = x_ref[i].astype(F32)
    loads[3].wait()
    pl.semaphore_wait(barrier, CTX - 1 + TP - 1 + 1)

    halo = copy(halo_out, halo_in, 0, {"ctx": peer_ctx(1)})
    halo.start()
    cot_copies = []
    for k in range(1, TP):
        c = copy(cot_all.at[tp], cot_all.at[tp], k, {"tp": peer_tp(k)})
        c.start()
        cot_copies.append(c)

    def send_filter(k, carry):
        peer = peer_nth(k)
        pltpu.make_async_remote_copy(
            filt_out.at[peer // 4], filt_in.at[ctx], all_snd.at[0], all_rcv.at[0],
            device_id={"ctx": peer}, device_id_type=MESH,
        ).start()
        return carry

    lax.fori_loop(0, CTX - 1, send_filter, 0)
    filt_in[pl.ds(ctx, 1)] = filt_out[pl.ds(ctx // 4, 1)]

    def wait_all(buf, n, which):
        pltpu.make_async_copy(buf.at[pl.ds(0, CTX - 1)], buf.at[pl.ds(0, CTX - 1)], which.at[n]).wait()

    halo.wait()
    loads[4].wait()
    loads[5].wait()

    for i in range(3):
        xe[i, 6:8, :] = halo_in[2 * i : 2 * i + 2, :]
    prev_seg = jnp.where(ctx == 0, -1.0, halo_in[6:8, 0:HALF])
    before1 = jnp.concatenate([prev_seg[1:2], seg_col[: ROWS - 1]], axis=0)
    before2 = jnp.concatenate([prev_seg, seg_col[: ROWS - 2]], axis=0)
    for n, before in enumerate((before1, before2)):
        mask = jnp.where(before == seg_col, 1.0, 0.0)
        masks[n] = jnp.concatenate([mask, mask], axis=1)

    def featurize(i):
        so[i] = (
            taps_ref[i, 0:1, :] * xe[i, 8 : 8 + ROWS, :]
            + taps_ref[i, 1:2, :] * masks[0] * xe[i, 7 : 7 + ROWS, :]
            + taps_ref[i, 2:3, :] * masks[1] * xe[i, 6 : 6 + ROWS, :]
        )

    featurize(1)
    featurize(2)

    def scatter(src, dst, n):
        def one(k, carry):
            peer = peer_nth(k)
            pltpu.make_async_remote_copy(
                src.at[peer], dst.at[ctx], all_snd.at[n], all_rcv.at[n],
                device_id={"ctx": peer}, device_id_type=MESH,
            ).start()
            return carry

        lax.fori_loop(0, CTX - 1, one, 0)
        dst[pl.ds(ctx, 1)] = src[pl.ds(ctx, 1)]

    def tiles_of(value):
        return (across(picks[0], value[:HALF]) + across(picks[1], value[HALF:])).reshape(CTX, 8, HALF).astype(BF)

    send_g[...] = tiles_of(plain(flips[0], (so[1] * so[2]).astype(BF)).astype(BF))
    scatter(send_g, recv_g, 1)
    featurize(0)

    wait_all(filt_in, 0, all_rcv)
    keep = rows128 >= cols128

    def spread(line):
        return pltpu.roll(jnp.broadcast_to(line, (HALF, HALF)), 1, 1, stride=1, stride_axis=0)

    def build(n, prev):
        for u in range(2):
            d = 2 * n + u
            line = filt_in[d]
            s0 = spread(line[:, :HALF])
            a0 = jnp.where(keep, s0, prev).astype(BF)
            s1_ = spread(line[:, HALF:])
            a1 = jnp.where(keep, s1_, s0).astype(BF)
            base = pl.multiple_of(d * 256, 256)
            toep[pl.ds(base, HALF), 0:HALF] = a0
            toep[pl.ds(base + HALF, HALF), HALF:COLS] = a0
            toep[pl.ds(base + HALF, HALF), 0:HALF] = a1
            toep[pl.ds(base + 256, HALF), HALF:COLS] = a1
            prev = s1_
        return prev

    toep[0:HALF, HALF:COLS] = jnp.zeros((HALF, HALF), BF)
    lax.fori_loop(0, 32, build, jnp.zeros((HALF, HALF), F32))

    for c in cot_copies:
        c.wait()
    total = across(cot_all[0], w_ref[:, 0:256])
    for i in range(1, TP):
        total += across(cot_all[i], w_ref[:, 256 * i : 256 * i + 256])
    gy[...] = total
    send_l[...] = tiles_of((total * so[0]).astype(BF))
    scatter(send_l, recv_l, 2)

    first3 = iota((32, 8, HALF), 1) < 4

    def swap4(value):
        return pltpu.roll(value, 4, 1)

    def halves(ref):
        both = ref[...].astype(F32).reshape(32, 16, HALF)
        return both[:, 0:8], both[:, 8:16]

    def rows_of(one, two):
        return jnp.concatenate(
            [jnp.where(first3, one, swap4(two)), jnp.where(first3, swap4(one), two)], axis=2
        ).reshape(256, COLS)

    def backwards(value):
        return jnp.concatenate([value[31 - i : 32 - i] for i in range(32)], axis=0)

    def convolve(rows):
        for e in range(4):
            if e:
                stacked[:, 256 * e : 256 * e + 256] = jnp.concatenate(
                    [jnp.zeros((4 * e, COLS), F32), rows[: 256 - 4 * e]], axis=0
                ).astype(BF)
            else:
                stacked[:, 0:256] = rows.astype(BF)
        for n in range(16):
            term = plain(stacked[0 : 256 - 16 * n, :], toep[1024 * n : 1024 * n + 1024, :])
            if n:
                acc[16 * n : 256, :] += term
            else:
                acc[...] = term
        done = acc[...].reshape(32, 8, COLS)
        low = done[:, :, :HALF]
        high = done[:, :, HALF:]
        return jnp.where(first3, low, swap4(high)), jnp.where(first3, swap4(low), high)

    def give(ref, one, two):
        ref[...] = jnp.concatenate([one, two], axis=1).reshape(CTX, 8, HALF).astype(BF)

    wait_all(recv_g, 1, all_rcv)
    even, odd = halves(recv_g)
    rows_g = rows_of(even, odd)
    one, two = convolve(rows_g)
    give(ret_f, one, two)
    scatter(ret_f, back_f, 3)
    gct[...] = jnp.transpose(rows_g).astype(BF)

    wait_all(recv_l, 2, all_rcv)
    even, odd = halves(recv_l)
    one, two = convolve(rows_of(backwards(odd), backwards(even)))
    give(ret_b, backwards(two), backwards(one))
    scatter(ret_b, back_b, 4)

    slot_t = iota((COLS, 512), 1)
    chan_t = iota((COLS, 512), 0)
    home_t = (slot_t // 8) * 4 + lax.rem(slot_t, 8)
    take_a = one_hot((home_t == chan_t) & (lax.rem(slot_t, 8) < 4))
    take_b = one_hot((home_t == chan_t + 4) & (lax.rem(slot_t, 8) >= 4))
    same = flips[1]

    def channels(ref):
        got = ref[...].astype(F32).reshape(512, HALF).astype(BF)
        return jnp.concatenate([plain(take_a, got), plain(take_b, got)], axis=1).astype(BF)

    wait_all(back_f, 3, all_rcv)
    long_out = across(flips[0], channels(back_f))
    y_all = so[0] * long_out
    y_hi = y_all.astype(BF)
    y_lo = (y_all - y_hi.astype(F32)).astype(BF)
    y_t[0] = across(same, y_hi).astype(BF)
    y_t[1] = across(same, y_lo).astype(BF)
    off = pl.multiple_of(other * HALF, HALF)
    mine = pl.multiple_of(dp * HALF, HALF)
    pair_copies = []
    for i in range(TP):
        pair_out[i] = (
            plain(y_t[0, pl.ds(off, HALF), :], cot_all[i]) + plain(y_t[1, pl.ds(off, HALF), :], cot_all[i])
        ).astype(BF)
        c = copy(pair_out.at[i], pair_in.at[i], 8 + i, {"dp": other})
        c.start()
        pair_copies.append(c)
    for i in range(TP):
        part[:, 256 * i : 256 * i + 256] = plain(y_t[0, pl.ds(mine, HALF), :], cot_all[i]) + plain(
            y_t[1, pl.ds(mine, HALF), :], cot_all[i]
        )
    mix_copies = []
    for i in range(TP):
        mix_out[i] = (
            plain(y_hi, w_ref[:, 256 * i : 256 * i + 256]) + plain(y_lo, w_ref[:, 256 * i : 256 * i + 256])
        ).astype(BF)
    for k in range(1, TP):
        c = copy(mix_out.at[peer_tp(k)], mix_in.at[tp], 4 + k, {"tp": peer_tp(k)})
        c.start()
        mix_copies.append(c)

    for i in range(TP):
        pair_copies[i].wait()
        both = part[:, 256 * i : 256 * i + 256] + pair_in[i].astype(F32)
        for r in range(8):
            for h in range(2):
                sum_out[8 * r + 2 * i + h] = both[16 * r : 16 * r + 16, HALF * h : HALF * h + HALF].astype(BF)
    scatter(sum_out, sum_in, 6)

    wait_all(back_b, 4, all_rcv)
    grad_gated = across(same, channels(back_b))
    edge_out[6:8, :] = jnp.zeros((2, COLS), F32)
    sm0[0, 9:16, :] = jnp.zeros((7, COLS), F32)
    for i in range(3):
        gso = (gy[...] * long_out, grad_gated * so[2], grad_gated * so[1])[i]
        z1 = gso * masks[0]
        z2 = gso * masks[1]
        f0, f1, f2 = (taps_ref[i, s : s + 1, :] for s in range(TAPS))
        edge_out[2 * i : 2 * i + 1, :] = f2 * z2[0:1]
        edge_out[2 * i + 1 : 2 * i + 2, :] = f1 * z1[0:1] + f2 * z2[1:2]
        zbuf[0, 0:ROWS, :] = z1
        zbuf[1, 0:ROWS, :] = z2
        zbuf[:, ROWS : ROWS + 8, :] = jnp.zeros((2, 8, COLS), F32)
        sm0[0, 3 * i : 3 * i + 1, :] = jnp.sum(gso * xe[i, 8 : 8 + ROWS, :], axis=0, keepdims=True)
        sm0[0, 3 * i + 1 : 3 * i + 2, :] = jnp.sum(z1 * xe[i, 7 : 7 + ROWS, :], axis=0, keepdims=True)
        sm0[0, 3 * i + 2 : 3 * i + 3, :] = jnp.sum(z2 * xe[i, 6 : 6 + ROWS, :], axis=0, keepdims=True)
        xe[i, 0:ROWS, :] = f0 * gso + f1 * zbuf[0, 1 : 1 + ROWS, :] + f2 * zbuf[1, 2 : 2 + ROWS, :]
    edge_copy = copy(edge_out, edge_in, 15, {"ctx": peer_ctx(CTX - 1)})
    edge_copy.start()
    small_pair = copy(sm0.at[0], sm0.at[1], 16, {"dp": other})
    small_pair.start()

    straight = rows_of(even, odd)
    next_even = jnp.concatenate([even[1:], jnp.zeros((1, 8, HALF), F32)], axis=0)
    crossed = rows_of(odd, next_even)
    zero8 = jnp.zeros((8, COLS), F32)
    for n, value in enumerate(
        (straight, crossed, jnp.concatenate([straight[8:], zero8], axis=0), jnp.concatenate([crossed[8:], zero8], axis=0))
    ):
        gls[n, 0:256, :] = value.astype(BF)
        gls[n, 256:512, :] = jnp.zeros((256, COLS), BF)
    later = cols128 > rows128

    def roll_up(block):
        return pltpu.roll(block, 1, 1, stride=1, stride_axis=0)

    def lag_row(now, last):
        return jnp.sum(jnp.where(later, now, last), axis=0, keepdims=True).reshape(1, 1, HALF)

    def correlate(width):
        def body(m, carry):
            c11, last = carry
            for u in range(4):
                c = plain(gct[:, 0:width], gls[u, pl.ds(pl.multiple_of(16 * m, 16), width), :])
                r0 = roll_up(c11 + c[:HALF, :HALF])
                r1 = roll_up(c[:HALF, HALF:] + c[HALF:, :HALF])
                lag_out[pl.ds(8 * m + 2 * u, 1)] = lag_row(r0, last)
                lag_out[pl.ds(8 * m + 2 * u + 1, 1)] = lag_row(r1, r0)
                c11 = c[HALF:, HALF:]
                last = r1
            return c11, last

        return body

    nothing = jnp.zeros((HALF, HALF), F32)

    c11, last = lax.fori_loop(0, 8, correlate(256), (nothing, nothing))
    small_pair.wait()
    sm1[0] = sm0[0] + sm0[1]
    small_first = []
    for k in range(1, 8):
        c = copy(sm1.at[0], sm1.at[k], 23 + k, dev1(k))
        c.start()
        small_first.append(c)
    c11, last = lax.fori_loop(8, 16, correlate(128), (c11, last))
    r0 = roll_up(c11)
    lag_out[128:129] = lag_row(r0, last)
    lag_out[129:130] = lag_row(nothing, r0)

    def send_lags(k, carry):
        peer = peer_nth(k)
        pltpu.make_async_remote_copy(
            lag_out.at[pl.ds(2 * peer + 2, 2)], lag_in.at[ctx], all_snd.at[5], all_rcv.at[5],
            device_id={"ctx": peer}, device_id_type=MESH,
        ).start()
        return carry

    lax.fori_loop(0, CTX - 1, send_lags, 0)
    lag_in[pl.ds(ctx, 1)] = lag_out[pl.ds(2 * ctx + 2, 2)].reshape(1, 2, 1, HALF)

    wait_all(sum_in, 6, all_rcv)
    total = sum_in[0].astype(F32)
    for n in range(1, CTX):
        total += sum_in[n].astype(F32)
    one_tile[...] = (total * scale).astype(BF)

    def share(k, carry):
        pltpu.make_async_remote_copy(
            one_tile, tiles.at[ctx], all_snd.at[7], grp.at[ctx // 16],
            device_id={"ctx": peer_nth(k)}, device_id_type=MESH,
        ).start()
        return carry

    lax.fori_loop(0, CTX - 1, share, 0)
    pltpu.make_async_copy(one_tile, tiles.at[ctx], grp.at[ctx // 16]).start()

    for c in small_first:
        c.wait()
    small = sm1[0]
    for k in range(1, 8):
        small += sm1[k]
    sm2[0] = small
    small_second = []
    for k in range(1, 8):
        c = copy(sm2.at[0], sm2.at[k], 38 + k, dev2(k))
        c.start()
        small_second.append(c)
    edge_copy.wait()
    for i in range(3):
        xe[i, ROWS - 2 : ROWS, :] += edge_in[2 * i : 2 * i + 2, :]
        gin_ref[i] = xe[i, 0:ROWS, :].astype(BF)
    for c in mix_copies:
        c.wait()
    total = mix_out[pl.ds(tp, 1)].astype(F32)
    for k in range(1, TP):
        total += mix_in[pl.ds(peer_tp(k), 1)].astype(F32)
    mixed_ref[...] = total.reshape(ROWS, COLS).astype(BF)
    wait_all(lag_in, 5, all_rcv)
    for g in range(16):
        for h in range(2):
            value = lag_in[4 * g, h] + lag_in[4 * g + 1, h] + lag_in[4 * g + 2, h] + lag_in[4 * g + 3, h]
            lag_pair[0, g : g + 1, HALF * h : HALF * h + HALF] = value
    lag_copy = copy(lag_pair.at[0], lag_pair.at[1], 31, {"dp": other})
    lag_copy.start()

    last_copies = []
    for q in range(4):
        group = pl.ds(16 * q, 16)
        pltpu.make_async_copy(tiles.at[group], tiles.at[group], grp.at[q]).wait()
        c = copy(tiles.at[group], tiles_in.at[group], 17 + q, {"dp": other})
        c.start()
        last_copies.append(c)
    for q in range(CTX):
        gproj_ref[pl.ds(pl.multiple_of(mine + 16 * (q // 8), 16), 16), HALF * (q % 8) : HALF * (q % 8) + HALF] = tiles[q]
    lag_copy.wait()
    glong_ref[...] = (lag_pair[0] + lag_pair[1]) * scale
    for c in small_second:
        c.wait()
    small = sm2[0]
    for k in range(1, 8):
        small += sm2[k]
    small = small * scale
    for i in range(3):
        gtaps_ref[i] = small[3 * i : 3 * i + 3, :]
    for n, buf in enumerate((filt_in, send_g, send_l, ret_f, ret_b, lag_in, sum_in, tiles)):
        wait_all(buf, n, all_snd)
    for c in last_copies:
        c.wait()
    for q in range(CTX):
        gproj_ref[pl.ds(pl.multiple_of(off + 16 * (q // 8), 16), 16), HALF * (q % 8) : HALF * (q % 8) + HALF] = tiles_in[q]


def store(mixed, gin, gtaps, glong, gproj, mixed_o, gin_o, gtaps_o, glong_o, gproj_o, wide, sem):
    copies = []
    for n, (src, dst) in enumerate(((gin, gin_o), (mixed, mixed_o), (glong, glong_o), (gtaps, gtaps_o))):
        c = pltpu.make_async_copy(src, dst, sem.at[n])
        c.start()
        copies.append(c)
    for n in range(2):
        rows = pl.ds(HALF * n, HALF)
        wide[rows, :] = gproj[rows, :].astype(F32)
        c = pltpu.make_async_copy(wide.at[rows, :], gproj_o.at[rows, :], sem.at[4 + n])
        c.start()
        copies.append(c)
    for c in copies:
        c.wait()


def per_device(projected, segment_ids, short_filter, long_filter, out_proj, mixed_cotangent):
    scale = 1.0 / math.sqrt(2 * ROWS * CTX)
    V = pltpu.VMEM
    spec = pl.BlockSpec(memory_space=pltpu.VMEM)
    mixed, grad_in, grad_taps, grad_long, grad_proj = pl.pallas_call(
        functools.partial(layer, scale),
        out_shape=(
            jax.ShapeDtypeStruct((ROWS, COLS), BF),
            jax.ShapeDtypeStruct((3, ROWS, COLS), BF),
            jax.ShapeDtypeStruct((3, TAPS, COLS), F32),
            jax.ShapeDtypeStruct((16, COLS), F32),
            jax.ShapeDtypeStruct((256, 1024), BF),
        ),
        in_specs=[pl.BlockSpec(memory_space=pltpu.HBM)] * 6,
        out_specs=[spec] * 5,
        scratch_shapes=[
            V((3, ROWS, COLS), BF), V((1, ROWS), jnp.int32), V((3, TAPS, COLS), F32), V((16, COLS), F32), V((256, 1024), BF),
            pltpu.SemaphoreType.DMA((6,)), V((2, 512, COLS), BF), V((2, ROWS, ROWS), BF),
            V((TP, ROWS, COLS), BF), V((8, COLS), F32), V((8, COLS), F32),
            V((16, 1, COLS), F32), V((CTX, 1, COLS), F32),
            V((3, ROWS + 8, COLS), F32), V((3, ROWS, COLS), F32), V((2, ROWS, COLS), F32), V((ROWS, COLS), F32),
            V((CTX, 8, HALF), BF), V((CTX, 8, HALF), BF), V((CTX, 8, HALF), BF), V((CTX, 8, HALF), BF),
            V((64 * 256 + 256, 256), BF), V((256, 1024), BF), V((256, 256), F32),
            V((256, 256), BF), V((4, 512, 256), BF), V((130, 1, HALF), F32), V((CTX, 2, 1, HALF), F32),
            V((CTX, 8, HALF), BF), V((CTX, 8, HALF), BF), V((CTX, 8, HALF), BF), V((CTX, 8, HALF), BF),
            V((2, ROWS + 8, COLS), F32), V((2, COLS, ROWS), BF), V((HALF, 1024), F32),
            V((TP, ROWS, COLS), BF), V((TP, ROWS, COLS), BF),
            V((TP, HALF, COLS), BF), V((TP, HALF, COLS), BF),
            V((CTX, 16, HALF), BF), V((CTX, 16, HALF), BF), V((16, HALF), BF), V((CTX, 16, HALF), BF), V((CTX, 16, HALF), BF),
            V((2, 16, COLS), F32), V((8, 16, COLS), F32), V((8, 16, COLS), F32),
            V((8, COLS), F32), V((8, COLS), F32), V((2, 16, COLS), F32),
            pltpu.SemaphoreType.DMA((46,)), pltpu.SemaphoreType.DMA((46,)),
            pltpu.SemaphoreType.DMA((8,)), pltpu.SemaphoreType.DMA((8,)), pltpu.SemaphoreType.DMA((4,)),
        ],
        compiler_params=pltpu.CompilerParams(vmem_limit_bytes=48 << 20, collective_id=0, has_side_effects=True),
        name="layer",
    )(*(pltpu.with_memory_space_constraint(v, pltpu.HBM) for v in (projected[:, 0], segment_ids, short_filter, long_filter, out_proj, mixed_cotangent[0])))
    mixed, grad_in, grad_taps, grad_long, grad_proj = pl.pallas_call(
        store,
        out_shape=(
            jax.ShapeDtypeStruct((ROWS, COLS), BF),
            jax.ShapeDtypeStruct((3, ROWS, COLS), BF),
            jax.ShapeDtypeStruct((3, TAPS, COLS), F32),
            jax.ShapeDtypeStruct((16, COLS), F32),
            jax.ShapeDtypeStruct((256, 1024), F32),
        ),
        in_specs=[spec] * 5,
        out_specs=[pl.BlockSpec(memory_space=pltpu.HBM)] * 5,
        scratch_shapes=[V((256, 1024), F32), pltpu.SemaphoreType.DMA((6,))],
        compiler_params=pltpu.CompilerParams(vmem_limit_bytes=8 << 20),
        name="store",
    )(mixed, grad_in, grad_taps, grad_long, grad_proj)
    return (mixed[None], grad_in[:, None], grad_taps, grad_long, grad_proj)


def solution(mesh):
    in_specs = (
        P(None, "dp", "ctx", "tp"),
        P("dp", "ctx"),
        P(None, None, "tp"),
        P("tp", "ctx"),
        P("tp", None),
        P("dp", "ctx", "tp"),
    )
    out_specs = (
        P("dp", "ctx", "tp"),
        P(None, "dp", "ctx", "tp"),
        P(None, None, "tp"),
        P("tp", "ctx"),
        P("tp", None),
    )
    return jax.shard_map(
        per_device, mesh=mesh, in_specs=in_specs, out_specs=out_specs, check_vma=False
    )
```
